128 devices in a mesh: req: 32 (over y, z, core), tp: 4 (over x).
Axes of the slice: x: 4, y: 4, z: 4, core: 2. Of those that a mesh axis runs over, the one named last changes fastest.
Arguments:
- tokens: bfloat16 [8192, 5120], P(('req', 'tp')), may hold values from -6 to 6
- norm_gain: bfloat16 [5120], replicated, may hold values from 0.099609375 to 1.8984375
- w_query: bfloat16 [5120, 2560], P(None, 'tp'), may hold values from -0.078125 to 0.078125
- w_key: bfloat16 [5120, 512], P(None, 'tp'), may hold values from -0.078125 to 0.078125
- w_value: bfloat16 [5120, 512], P(None, 'tp'), may hold values from -0.078125 to 0.078125
- query_gain: bfloat16 [128], replicated, may hold values from 0.25 to 1.75
- key_gain: bfloat16 [128], replicated, may hold values from 2 to 5
- w_out: bfloat16 [2560, 5120], P('tp'), may hold values from -0.125 to 0.125
- cache_keys: bfloat16 [524288, 512], P('req', 'tp'), may hold values from -91 to 91
- cache_values: bfloat16 [524288, 512], P('req', 'tp'), may hold values from -6 to 6
- cache_plan: int32 [32, 8], replicated, may hold values from 0 to 2048, as said below
Outputs:
- mixed: bfloat16 [8192, 5120], P(('req', 'tp'))
The draws below stay inside these ranges and needn't reach their ends.
Inputs may be any that keep to these rules, and one draw needn't show every extreme that they name: `cache_plan`: row r holds the sizes of the 8 pieces of request r's cache, piece k kept on request-axis device (r + k) mod 32. A cache holds either at most 384 tokens or at least 14336; no piece exceeds 2048, and some request's cache has all its pieces full.
All inputs are finite; a program needn't handle non-finite values.
Results may differ from the reference program's by a relative error of at most 0.025.
Values may be sent and summed in bfloat16 or wider, within the bound.
A program may use at most 128 MiB of HBM per device.

```python
import math
import jax
import jax.numpy as jnp
from jax import lax

D = 5120
HEADS = 20
KVH = 4
HD = 128
NEW = 256
SPREAD = 8
LONG = 16384
SHORT = 256
SEGCAP = 2048
REQS = 32
TOKENS = 8192
POOL = 524288
N_REQ = 32
N_TP = 4


def draw_cache_plan(key, part):
    key_long, key_pick, key_len, key_short, key_weight = jax.random.split(key, 5)
    long_flag = jax.random.randint(key_long, (REQS,), 0, 2) == 1
    forced = jax.random.randint(key_pick, (), 0, REQS)
    is_forced = jnp.arange(REQS) == forced
    long_flag = long_flag | is_forced
    long_len = jax.random.randint(key_len, (REQS,), LONG - SEGCAP, LONG + 1)
    long_len = jnp.where(is_forced, LONG, long_len)
    short_len = jax.random.randint(key_short, (REQS,), SHORT // 2, 3 * SHORT // 2 + 1)
    shares = jax.random.randint(key_weight, (REQS, SPREAD), 1, 9)
    share_sum = jnp.sum(shares, axis=1, keepdims=True)
    short_pieces = short_len[:, None] * shares // share_sum
    short_pieces = short_pieces.at[:, 0].add(short_len - jnp.sum(short_pieces, axis=1))
    deficit = SPREAD * SEGCAP - long_len
    cuts = deficit[:, None] * shares // share_sum
    cuts = cuts.at[:, 0].add(deficit - jnp.sum(cuts, axis=1))
    long_pieces = SEGCAP - cuts
    return jnp.where(long_flag[:, None], long_pieces, short_pieces).astype(jnp.int32)


def draw_cache_keys(key, part):
    key_base, key_gain, key_pos = jax.random.split(key, 3)
    base = jax.random.normal(key_base, (POOL, KVH, HD), jnp.float32)
    normed = base * jax.lax.rsqrt(jnp.mean(base * base, axis=-1, keepdims=True) + 1e-06)
    gains = jnp.exp(math.log(2.0) + jax.random.uniform(key_gain, (POOL, KVH, HD), jnp.float32) * math.log(4.0))
    scaled = normed * gains
    positions = jax.random.randint(key_pos, (POOL, 1, 1), 0, LONG).astype(jnp.float32)
    freqs = 1000000.0 ** (-(jnp.arange(HD // 2).astype(jnp.float32) * 2.0) / HD)
    angles = positions * freqs[None, None, :]
    leading = scaled[..., :HD // 2]
    trailing = scaled[..., HD // 2:]
    rotated = jnp.concatenate([leading * jnp.cos(angles) - trailing * jnp.sin(angles), trailing * jnp.cos(angles) + leading * jnp.sin(angles)], axis=-1)
    return jnp.clip(rotated, -90.0, 90.0).reshape(POOL, KVH * HD).astype(jnp.bfloat16)


def levels(rng, dims, pieces, least, largest):
    factor_of = 1.0
    for axis_at, shards_of in pieces:
        heights = jax.random.uniform(jax.random.fold_in(jax.random.fold_in(rng, 6), axis_at), (shards_of,), jnp.float32, least / len(pieces), largest / len(pieces))
        factor_of = factor_of * jnp.repeat(jnp.exp(heights), dims[axis_at] // shards_of).reshape((-1,) + (1,) * (len(dims) - 1 - axis_at))
    return factor_of


def scatter_about(own_key, dims, scale, bound, shards=(), dtype=jnp.bfloat16):
    array = scale * jax.random.normal(own_key, dims, jnp.float32)
    if shards:
        array = array * levels(own_key, dims, shards, -0.22, 0.18)
    return jnp.clip(array, -bound, bound).astype(dtype)


def setup_inputs(seed: int = 0) -> dict:
    streams_of = jax.random.split(jax.random.key(seed), 12)
    tokens = scatter_about(streams_of[0], (TOKENS, D), 1.0, 6.0, ((0, 128),))
    norm_gain = jnp.clip(1.0 + 0.18 * jax.random.normal(streams_of[1], (D,), jnp.float32), 0.099609375, 1.8984375).astype(jnp.bfloat16)
    w_query = scatter_about(streams_of[2], (D, HEADS * HD), D ** -0.5, 0.078125, ((1, 4),))
    w_key = scatter_about(streams_of[3], (D, KVH * HD), D ** -0.5, 0.078125, ((1, 4),))
    w_value = scatter_about(streams_of[4], (D, KVH * HD), D ** -0.5, 0.078125, ((1, 4),))
    query_gain = jnp.clip(1.0 + 0.15 * jax.random.normal(streams_of[5], (HD,), jnp.float32), 0.25, 1.75).astype(jnp.bfloat16)
    key_gain = jnp.clip(jnp.exp(jax.random.uniform(streams_of[6], (HD,), jnp.float32, math.log(2.0), math.log(5.0))), 2.0, 5.0).astype(jnp.bfloat16)
    w_out = scatter_about(streams_of[7], (HEADS * HD, D), (HEADS * HD) ** -0.5, 0.125, ((0, 4),))
    cache_keys = draw_cache_keys(jax.random.fold_in(streams_of[11], 71), 0)
    cache_values = scatter_about(streams_of[9], (POOL, KVH * HD), 1.0, 6.0, ((0, 32), (1, 4)))
    cache_plan = draw_cache_plan(jax.random.fold_in(streams_of[11], 71), 0)
    return {"tokens": tokens, "norm_gain": norm_gain, "w_query": w_query, "w_key": w_key, "w_value": w_value, "query_gain": query_gain, "key_gain": key_gain, "w_out": w_out, "cache_keys": cache_keys, "cache_values": cache_values, "cache_plan": cache_plan}


norm_eps = 1e-06
rope_base = 1000000.0

def rms_scale(values, gain):
    return values * lax.rsqrt(lax.optimization_barrier(jnp.mean(values * values, axis=-1, keepdims=True)) + norm_eps) * gain.astype(jnp.float32)

def rotate(values, angles):
    half_dim = values.shape[-1] // 2
    cosine = jnp.cos(angles)
    sine_part = jnp.sin(angles)
    leading = values[..., :half_dim]
    trailing = values[..., half_dim:]
    return jnp.concatenate([leading * cosine - trailing * sine_part, trailing * cosine + leading * sine_part], axis=-1)

def reference(tokens, norm_gain, w_query, w_key, w_value, query_gain, key_gain, w_out, cache_keys, cache_values, cache_plan):
    token_rows = tokens.astype(jnp.float32)
    normed = rms_scale(token_rows, norm_gain).astype(jnp.bfloat16)
    query_all = jnp.dot(normed, w_query, preferred_element_type=jnp.float32).reshape(REQS, NEW, HEADS, HD)
    key_all = jnp.dot(normed, w_key, preferred_element_type=jnp.float32).reshape(REQS, NEW, KVH, HD)
    value_all = jnp.dot(normed, w_value, preferred_element_type=jnp.float32).astype(jnp.bfloat16).reshape(REQS, NEW, KVH, HD)
    lengths = lax.optimization_barrier(jnp.sum(cache_plan, axis=1))
    positions = (lengths[:, None] + jnp.arange(NEW)[None, :]).astype(jnp.float32)
    freqs = rope_base ** (-(jnp.arange(HD // 2).astype(jnp.float32) * 2.0) / HD)
    angles = (positions[:, :, None] * freqs[None, None, :])[:, :, None, :]
    queries = rotate(rms_scale(query_all, query_gain), angles).astype(jnp.bfloat16)
    new_keys = rotate(rms_scale(key_all, key_gain), angles).astype(jnp.bfloat16)
    group_size = HEADS // KVH
    score_scale = HD ** (-0.5)
    causal = jnp.arange(NEW)[:, None] >= jnp.arange(NEW)[None, :]

    def attend_one(inputs):
        index, query_block, key_block, value_block, counts = inputs
        gathered_keys = []
        gathered_values = []
        for k in range(SPREAD):
            first_row = ((index + k) % N_REQ * LONG + k * SEGCAP).astype(jnp.int32)
            gathered_keys.append(lax.dynamic_slice_in_dim(cache_keys, first_row, SEGCAP, 0))
            gathered_values.append(lax.dynamic_slice_in_dim(cache_values, first_row, SEGCAP, 0))
        cached = (jnp.arange(SEGCAP)[None, :] < counts[:, None]).reshape(SPREAD * SEGCAP)
        all_keys = jnp.concatenate(gathered_keys + [key_block.reshape(NEW, KVH * HD)], axis=0)
        all_keys = all_keys.reshape(-1, KVH, HD).astype(jnp.float32)
        all_values = jnp.concatenate(gathered_values + [value_block.reshape(NEW, KVH * HD)], axis=0)
        all_values = all_values.reshape(-1, KVH, HD).astype(jnp.float32)
        visible = jnp.concatenate([jnp.broadcast_to(cached[None, :], (NEW, SPREAD * SEGCAP)), causal], axis=1)
        visible = visible[:, None, None, :]
        grouped = query_block.astype(jnp.float32).reshape(NEW, KVH, group_size, HD)
        scores = jnp.einsum('tkgd,skd->tkgs', grouped, all_keys) * score_scale
        scores = jnp.where(visible, scores, -jnp.inf)
        highest = lax.optimization_barrier(jnp.max(scores, axis=-1, keepdims=True))
        weights = jnp.where(visible, jnp.exp(scores - highest), 0.0)
        total_mass = lax.optimization_barrier(jnp.sum(weights, axis=-1))
        rounded = lax.optimization_barrier(weights.astype(jnp.bfloat16)).astype(jnp.float32)
        weighted = jnp.einsum('tkgs,skd->tkgd', rounded, all_values)
        return (weighted / total_mass[..., None]).astype(jnp.bfloat16).reshape(NEW, HEADS * HD)
    attended = lax.map(attend_one, (jnp.arange(REQS).astype(jnp.int32), queries, new_keys, value_all, cache_plan))
    attended = attended.reshape(TOKENS, HEADS * HD)
    width = HEADS * HD // N_TP
    summed = jnp.zeros((TOKENS, D), jnp.float32)
    for g in range(N_TP):
        partial_term = jnp.dot(attended[:, g * width:(g + 1) * width], w_out[g * width:(g + 1) * width], preferred_element_type=jnp.float32)
        summed = summed + lax.optimization_barrier(partial_term.astype(jnp.bfloat16)).astype(jnp.float32)
    return (token_rows + summed).astype(jnp.bfloat16)
```

```python
import functools
import jax
import jax.numpy as jnp
from jax import lax
from jax.experimental import pallas as pl
from jax.experimental.pallas import tpu as pltpu
from jax.sharding import PartitionSpec as P

norm_eps = 1e-06
rope_base = 1000000.0
log2e = 1.4426950408889634

NEG = -1e30

def softmax_pv(qs, kx, vx, causal=False, order=0):
    outs = []
    def sc(q):
        s = lax.dot_general(q, kx, (((1,), (1,)), ((), ())), preferred_element_type=jnp.float32)
        if causal:
            r = lax.broadcasted_iota(jnp.int32, s.shape, 0); c = lax.broadcasted_iota(jnp.int32, s.shape, 1)
            s = jnp.where(r >= c, s, NEG)
        return s
    ss = [sc(q) for q in qs] if order == 1 else None
    for i, q in enumerate(qs):
        s = ss[i] if ss else sc(q)
        m = jnp.max(s, axis=1, keepdims=True)
        p = jnp.exp2(s - m).astype(jnp.bfloat16)
        oe = jnp.dot(p, vx, preferred_element_type=jnp.float32)
        l = oe[:, 128:]
        outs.append((oe[:, :128] / l, m + jnp.log2(l)))
    return outs

def attn_kernel(order, heads, held_ref, q_ref, k_ref, v_ref, nk_ref, nv_ref, o_ref, st_ref, kx_ref, vx_ref):
    j = pl.program_id(0)
    n = pl.num_programs(0)
    hd = 128
    T = q_ref.shape[1]
    lanes = lax.broadcasted_iota(jnp.int32, (T, hd), 1)

    def emit(outs):
        st = jnp.full((T, hd), NEG, jnp.float32)
        for g, (o, lse) in enumerate(outs):
            o_ref[0, :, g * hd:(g + 1) * hd] = o.astype(jnp.bfloat16)
            st = jnp.where(lanes == g, lse, st)
        st_ref[0] = jnp.transpose(st)[:8]

    def run(length, held):
        rows = lax.broadcasted_iota(jnp.int32, (length, hd), 0)
        ok = rows < held
        kx_ref[:length] = jnp.where(ok, k_ref[:length], jnp.broadcast_to(k_ref[0:1], (length, hd)))
        vx_ref[:length, :hd] = jnp.where(ok, v_ref[:length], jnp.zeros((length, hd), jnp.bfloat16))
        vx_ref[:length, hd:] = jnp.where(ok, 1.0, 0.0).astype(jnp.bfloat16)
        qs = [q_ref[0, :, g * hd:(g + 1) * hd] for g in range(heads)]
        emit(softmax_pv(qs, kx_ref[:length], vx_ref[:length], order=order))

    held = held_ref[jnp.minimum(j, n - 2)]
    full = k_ref.shape[0]
    small = min(full, 512)

    @pl.when(jnp.logical_and(j < n - 1, held > small))
    def _():
        run(full, held)

    @pl.when(jnp.logical_and(j < n - 1, jnp.logical_and(held > 0, held <= small)))
    def _():
        run(small, held)

    @pl.when(jnp.logical_and(j < n - 1, held <= 0))
    def _():
        o_ref[...] = jnp.zeros_like(o_ref)
        st_ref[...] = jnp.full_like(st_ref, NEG)

    @pl.when(j == n - 1)
    def _():
        kx_ref[:T] = nk_ref[...]
        vx_ref[:T, :hd] = nv_ref[...]
        vx_ref[:T, hd:] = jnp.ones((T, hd), jnp.bfloat16)
        qs = [q_ref[0, :, g * hd:(g + 1) * hd] for g in range(heads)]
        emit(softmax_pv(qs, kx_ref[:T], vx_ref[:T], causal=True, order=order))

def attn(held, q, k, v, nk, nv, order=1):
    spread, T, W = q.shape
    hd = k.shape[1]
    cap = k.shape[0] // spread
    return pl.pallas_call(
        functools.partial(attn_kernel, order, W // hd),
        out_shape=(jax.ShapeDtypeStruct((spread + 1, T, W), jnp.bfloat16),
                   jax.ShapeDtypeStruct((spread + 1, 8, T), jnp.float32)),
        grid_spec=pltpu.PrefetchScalarGridSpec(
            num_scalar_prefetch=1, grid=(spread + 1,),
            in_specs=[
                pl.BlockSpec((1, T, W), lambda j, h: (lax.rem(j, spread), 0, 0)),
                pl.BlockSpec((cap, hd), lambda j, h: (jnp.minimum(j, spread - 1), 0)),
                pl.BlockSpec((cap, hd), lambda j, h: (jnp.minimum(j, spread - 1), 0)),
                pl.BlockSpec((T, hd), lambda j, h: (0, 0)),
                pl.BlockSpec((T, hd), lambda j, h: (0, 0)),
            ],
            out_specs=[pl.BlockSpec((1, T, W), lambda j, h: (j, 0, 0)),
                       pl.BlockSpec((1, 8, T), lambda j, h: (j, 0, 0))],
            scratch_shapes=[pltpu.VMEM((cap, hd), jnp.bfloat16), pltpu.VMEM((cap, 2 * hd), jnp.bfloat16)],
        ),
        compiler_params=pltpu.CompilerParams(vmem_limit_bytes=60 * 1024 * 1024),
    )(held, q, k, v, nk, nv)


def shifted(value, axis, steps):
    count = lax.axis_size(axis)
    pairs = [(source, (source + steps) % count) for source in range(count)]
    return lax.ppermute(value, axis, pairs)


def rms_scale(values, gain):
    return (
        values
        * lax.rsqrt(jnp.mean(values * values, axis=-1, keepdims=True) + norm_eps)
        * gain.astype(jnp.float32)
    )


def rotate(values, angles):
    half_dim = values.shape[-1] // 2
    cosine = jnp.cos(angles)
    sine_part = jnp.sin(angles)
    leading = values[..., :half_dim]
    trailing = values[..., half_dim:]
    return jnp.concatenate(
        [leading * cosine - trailing * sine_part, trailing * cosine + leading * sine_part], axis=-1
    )


def on_device(
    tokens,
    norm_gain,
    w_query,
    w_key,
    w_value,
    query_gain,
    key_gain,
    w_out,
    cache_keys,
    cache_values,
    cache_plan,
):
    head_dim = query_gain.shape[0]
    q_width = w_query.shape[1]
    q_heads = q_width // head_dim
    requests, spread = cache_plan.shape
    score_scale = head_dim ** (-0.5) * log2e
    device = lax.axis_index("req")
    lengths = jnp.sum(cache_plan, axis=1)
    req_ids = jnp.arange(requests)
    own_length = jnp.sum(jnp.where(req_ids == device, lengths, 0))
    owners = (device - jnp.arange(spread)) % requests
    held = jnp.sum(jnp.where(req_ids[None, :] == owners[:, None], cache_plan.T, 0), axis=1)
    token_rows = tokens.astype(jnp.float32)
    normed = rms_scale(token_rows, norm_gain).astype(jnp.bfloat16)
    piece_rows = lax.all_gather(normed, "tp", axis=0, tiled=True)
    proj_q = jnp.dot(piece_rows, w_query, preferred_element_type=jnp.float32)
    proj_k = jnp.dot(piece_rows, w_key, preferred_element_type=jnp.float32)
    new_values = jnp.dot(piece_rows, w_value, preferred_element_type=jnp.float32).astype(
        jnp.bfloat16
    )
    count_new = proj_q.shape[0]
    positions = (own_length + jnp.arange(count_new)).astype(jnp.float32)
    freqs = rope_base ** (-(jnp.arange(head_dim // 2).astype(jnp.float32) * 2.0) / head_dim)
    angles = positions[:, None] * freqs[None, :]
    query_heads = proj_q.reshape(count_new, q_heads, head_dim)
    queries = rotate(rms_scale(query_heads, query_gain), angles[:, None, :]) * score_scale
    queries = queries.astype(jnp.bfloat16).reshape(count_new, q_width)
    new_keys = rotate(rms_scale(proj_k, key_gain), angles).astype(jnp.bfloat16)
    arrived = [queries] + [shifted(queries, "req", k) for k in range(1, spread)]
    parts, stats = attn(
        held, jnp.stack(arrived), cache_keys, cache_values, new_keys, new_values
    )
    outs = [parts[spread], parts[0]]
    tops = [stats[spread], stats[0]]
    for k in range(1, spread):
        outs.append(shifted(parts[k], "req", -k))
        tops.append(shifted(stats[k], "req", -k))
    tops = jnp.stack(tops)[:, :q_heads]
    shares = jnp.exp2(tops - jnp.max(tops, axis=0, keepdims=True))
    shares = shares / jnp.sum(shares, axis=0, keepdims=True)
    attended = sum(
        out.astype(jnp.float32).reshape(count_new, q_heads, head_dim)
        * shares[i].T[:, :, None]
        for i, out in enumerate(outs)
    )
    attended = attended.reshape(count_new, q_width).astype(jnp.bfloat16)
    summed = lax.psum_scatter(
        jnp.dot(attended, w_out, preferred_element_type=jnp.float32).astype(jnp.bfloat16),
        "tp",
        scatter_dimension=0,
        tiled=True,
    ).astype(jnp.float32)
    return (token_rows + summed).astype(jnp.bfloat16)


def solution(mesh):
    placed = (
        P(("req", "tp"), None),
        P(),
        P(None, "tp"),
        P(None, "tp"),
        P(None, "tp"),
        P(),
        P(),
        P("tp", None),
        P("req", "tp"),
        P("req", "tp"),
        P(),
    )
    return jax.shard_map(
        on_device, mesh=mesh, in_specs=placed, out_specs=P(("req", "tp"), None), check_vma=False
    )
```

```python
import functools
import jax
import jax.numpy as jnp
from jax import lax
from jax.experimental import pallas as pl
from jax.experimental.pallas import tpu as pltpu
from jax.sharding import PartitionSpec as P

norm_eps = 1e-06
rope_base = 1000000.0
log2e = 1.4426950408889634

NEG = -1e30

def softmax_pv(qs, kx, vx, causal=False, order=0):
    outs = []
    def sc(q):
        s = lax.dot_general(q, kx, (((1,), (1,)), ((), ())), preferred_element_type=jnp.float32)
        if causal:
            r = lax.broadcasted_iota(jnp.int32, s.shape, 0); c = lax.broadcasted_iota(jnp.int32, s.shape, 1)
            s = jnp.where(r >= c, s, NEG)
        return s
    ss = [sc(q) for q in qs] if order == 1 else None
    for i, q in enumerate(qs):
        s = ss[i] if ss else sc(q)
        m = jnp.max(s, axis=1, keepdims=True)
        p = jnp.exp2(s - m).astype(jnp.bfloat16)
        oe = jnp.dot(p, vx, preferred_element_type=jnp.float32)
        l = oe[:, 128:]
        outs.append((oe[:, :128] / l, m + jnp.log2(l)))
    return outs

def attn_kernel(order, heads, held_ref, q_ref, k_ref, v_ref, nk_ref, nv_ref, o_ref, st_ref, kx_ref, vx_ref):
    j = pl.program_id(0)
    n = pl.num_programs(0)
    hd = 128
    T = q_ref.shape[1]
    lanes = lax.broadcasted_iota(jnp.int32, (T, hd), 1)

    def emit(outs):
        st = jnp.full((T, hd), NEG, jnp.float32)
        for g, (o, lse) in enumerate(outs):
            o_ref[0, :, g * hd:(g + 1) * hd] = o.astype(jnp.bfloat16)
            st = jnp.where(lanes == g, lse, st)
        st_ref[0] = jnp.transpose(st)[:8]

    def run(length, held):
        rows = lax.broadcasted_iota(jnp.int32, (length, hd), 0)
        ok = rows < held
        kx_ref[:length] = jnp.where(ok, k_ref[:length], jnp.broadcast_to(k_ref[0:1], (length, hd)))
        vx_ref[:length, :hd] = jnp.where(ok, v_ref[:length], jnp.zeros((length, hd), jnp.bfloat16))
        vx_ref[:length, hd:] = jnp.where(ok, 1.0, 0.0).astype(jnp.bfloat16)
        qs = [q_ref[0, :, g * hd:(g + 1) * hd] for g in range(heads)]
        emit(softmax_pv(qs, kx_ref[:length], vx_ref[:length], order=order))

    held = held_ref[jnp.minimum(j, n - 2)]
    full = k_ref.shape[0]
    small = min(full, 512)

    @pl.when(jnp.logical_and(j < n - 1, held > small))
    def _():
        run(full, held)

    @pl.when(jnp.logical_and(j < n - 1, jnp.logical_and(held > 0, held <= small)))
    def _():
        run(small, held)

    @pl.when(jnp.logical_and(j < n - 1, held <= 0))
    def _():
        o_ref[...] = jnp.zeros_like(o_ref)
        st_ref[...] = jnp.full_like(st_ref, NEG)

    @pl.when(j == n - 1)
    def _():
        kx_ref[:T] = nk_ref[...]
        vx_ref[:T, :hd] = nv_ref[...]
        vx_ref[:T, hd:] = jnp.ones((T, hd), jnp.bfloat16)
        qs = [q_ref[0, :, g * hd:(g + 1) * hd] for g in range(heads)]
        emit(softmax_pv(qs, kx_ref[:T], vx_ref[:T], causal=True, order=order))

def attn(held, q, k, v, nk, nv, order=1):
    spread, T, W = q.shape
    hd = k.shape[1]
    cap = k.shape[0] // spread
    return pl.pallas_call(
        functools.partial(attn_kernel, order, W // hd),
        out_shape=(jax.ShapeDtypeStruct((spread + 1, T, W), jnp.bfloat16),
                   jax.ShapeDtypeStruct((spread + 1, 8, T), jnp.float32)),
        grid_spec=pltpu.PrefetchScalarGridSpec(
            num_scalar_prefetch=1, grid=(spread + 1,),
            in_specs=[
                pl.BlockSpec((1, T, W), lambda j, h: (lax.rem(j, spread), 0, 0)),
                pl.BlockSpec((cap, hd), lambda j, h: (jnp.minimum(j, spread - 1), 0)),
                pl.BlockSpec((cap, hd), lambda j, h: (jnp.minimum(j, spread - 1), 0)),
                pl.BlockSpec((T, hd), lambda j, h: (0, 0)),
                pl.BlockSpec((T, hd), lambda j, h: (0, 0)),
            ],
            out_specs=[pl.BlockSpec((1, T, W), lambda j, h: (j, 0, 0)),
                       pl.BlockSpec((1, 8, T), lambda j, h: (j, 0, 0))],
            scratch_shapes=[pltpu.VMEM((cap, hd), jnp.bfloat16), pltpu.VMEM((cap, 2 * hd), jnp.bfloat16)],
        ),
        compiler_params=pltpu.CompilerParams(vmem_limit_bytes=60 * 1024 * 1024),
    )(held, q, k, v, nk, nv)


MESH = pl.DeviceIdType.MESH


def remote(src, dst, send, recv, req, tp):
    return pltpu.make_async_remote_copy(
        src_ref=src,
        dst_ref=dst,
        send_sem=send,
        recv_sem=recv,
        device_id=(req, tp),
        device_id_type=MESH,
    )


def greet(partners):
    barrier = pltpu.get_barrier_semaphore()
    for where in partners:
        pl.semaphore_signal(barrier, inc=1, device_id=where, device_id_type=MESH)
    pl.semaphore_wait(barrier, len(partners))


def spots():
    req, tp = lax.axis_index("req"), lax.axis_index("tp")
    n_tp = lax.axis_size("tp")
    core = lax.rem(req, 2)
    z = lax.rem(req // 2, 4)
    plane = req - 2 * z - core
    n_req = lax.axis_size("req")
    return req, tp, n_tp, n_req, core, z, plane


def project_kernel(
    score_scale,
    tok_ref,
    gain_ref,
    wq_ref,
    wk_ref,
    wv_ref,
    qg_ref,
    kg_ref,
    cos_ref,
    sin_ref,
    all_ref,
    nk_ref,
    nv_ref,
    xs,
    w,
    acc,
    qbuf,
    ag_send,
    ag_recv,
    y_send,
    y_recv,
    z_send,
    z_recv,
    d_send,
    d_recv,
    f_send,
    f_recv,
    w_sem,
    own_sem,
):
    req, tp, n_tp, n_req, core, z, plane = spots()
    rows = tok_ref.shape[0]
    half = rows // 2
    hd = qg_ref.shape[1]
    qw = wq_ref.shape[1]
    heads = qw // hd
    depth = tok_ref.shape[1]
    right, left = lax.rem(tp + 1, n_tp), lax.rem(tp + n_tp - 1, n_tp)
    y_next, y_prev = lax.rem(req + 8, n_req), lax.rem(req + n_req - 8, n_req)
    mate = req + 1 - 2 * core

    def z_peer(dz):
        return plane + 2 * lax.rem(z + dz, 4) + core

    w_copies = [
        pltpu.make_async_copy(wq_ref, w.at[:, :qw], w_sem.at[0]),
        pltpu.make_async_copy(wk_ref, w.at[:, qw : qw + hd], w_sem.at[1]),
        pltpu.make_async_copy(wv_ref, w.at[:, qw + hd :], w_sem.at[2]),
    ]
    for copy in w_copies:
        copy.start()
    greet(
        [(req, right), (req, left), (y_next, tp), (y_prev, tp), (mate, tp)]
        + [(z_peer(dz), tp) for dz in (1, 2, 3)]
    )
    tok = tok_ref[...].astype(jnp.float32)
    scale = lax.rsqrt(jnp.mean(tok * tok, axis=-1, keepdims=True) + norm_eps)
    xs[0] = (tok * scale * gain_ref[...].astype(jnp.float32)).astype(jnp.bfloat16)

    low, high = slice(0, half), slice(half, rows)

    def ag(index, slot_from, slot_to, part, target):
        return remote(
            xs.at[slot_from, part],
            xs.at[slot_to, part],
            ag_send.at[index],
            ag_recv.at[index],
            req,
            target,
        )

    ag_copies = [
        ag(0, 0, 1, low, right),
        ag(1, 0, 3, high, left),
        ag(2, 0, 1, high, right),
        ag(3, 0, 3, low, left),
        ag(4, 1, 2, low, right),
        ag(5, 3, 2, high, left),
    ]
    for copy in ag_copies[:4]:
        copy.start()
    for copy in w_copies:
        copy.wait()

    def first_row(s):
        return pl.multiple_of(lax.rem(tp + n_tp - s, n_tp) * rows, rows)

    def slot_rows(k, s):
        return all_ref.at[k, pl.ds(first_row(s), rows), :]

    def y_copy(s):
        return remote(qbuf.at[0, s], qbuf.at[1, s], y_send.at[s], y_recv.at[s], y_next, tp)

    def z_copy(dz, s):
        return remote(
            qbuf.at[(z + dz) // 4, s],
            slot_rows(2 * dz, s),
            z_send.at[dz - 1, s],
            z_recv.at[dz - 1, s],
            z_peer(dz),
            tp,
        )

    def d_copy(s):
        return remote(
            qbuf.at[core, s], slot_rows(1 + 6 * core, s), d_send.at[s], d_recv.at[s], mate, tp
        )

    def f_copy(dz, s):
        return remote(
            slot_rows(2 * dz, s),
            slot_rows(2 * dz + 1 - 2 * core, s),
            f_send.at[dz - 1, s],
            f_recv.at[dz - 1, s],
            mate,
            tp,
        )

    def own_copy(s):
        return pltpu.make_async_copy(qbuf.at[0, s], slot_rows(0, s), own_sem.at[s])

    def stage(s):
        acc[...] = jnp.zeros_like(acc)
        width = depth // 5

        def block(b, carry):
            at = pl.ds(pl.multiple_of(b * width, width), width)
            acc[...] += jnp.dot(xs[s, :, at], w[at, :], preferred_element_type=jnp.float32)
            return carry

        lax.fori_loop(0, 5, block, 0)
        here = pl.ds(first_row(s), rows)
        cosine, sine = cos_ref[here, :], sin_ref[here, :]

        def turned(at, gain):
            head = acc[:, at : at + hd]
            head = head * lax.rsqrt(jnp.mean(head * head, axis=-1, keepdims=True) + norm_eps) * gain
            return head * cosine + pltpu.roll(head, hd // 2, 1) * sine

        q_gain = qg_ref[...].astype(jnp.float32) * score_scale
        for h in range(heads):
            qbuf[0, s, :, h * hd : (h + 1) * hd] = turned(h * hd, q_gain).astype(jnp.bfloat16)
        nk_ref[here, :] = turned(qw, kg_ref[...].astype(jnp.float32)).astype(jnp.bfloat16)
        nv_ref[here, :] = acc[:, qw + hd :].astype(jnp.bfloat16)
        y_copy(s).start()
        for dz in (1, 2, 3):

            @pl.when(z + dz < 4)
            def _():
                z_copy(dz, s).start()

        @pl.when(core == 0)
        def _():
            d_copy(s).start()

        own_copy(s).start()

    def relay(s):
        y_copy(s).wait_recv()
        for dz in (1, 2, 3):

            @pl.when(z + dz >= 4)
            def _():
                z_copy(dz, s).start()

        @pl.when(core == 1)
        def _():
            d_copy(s).start()

    def pass_on(s):
        for dz in (1, 2, 3):
            z_copy(dz, s).wait_recv()
            f_copy(dz, s).start()

    stage(0)
    ag_copies[0].wait_recv()
    ag_copies[4].start()
    ag_copies[1].wait_recv()
    ag_copies[5].start()
    relay(0)
    ag_copies[2].wait_recv()
    stage(1)
    ag_copies[3].wait_recv()
    pass_on(0)
    stage(3)
    relay(1)
    relay(3)
    ag_copies[4].wait_recv()
    ag_copies[5].wait_recv()
    stage(2)
    pass_on(1)
    pass_on(3)
    relay(2)
    pass_on(2)
    for s in range(4):
        d_copy(s).wait_recv()
        for dz in (1, 2, 3):
            f_copy(dz, s).wait_recv()
    for copy in ag_copies:
        copy.wait_send()
    for s in range(4):
        own_copy(s).wait()
        y_copy(s).wait_send()
        d_copy(s).wait_send()
        for dz in (1, 2, 3):
            z_copy(dz, s).wait_send()
            f_copy(dz, s).wait_send()


def project(tokens, norm_gain, w_query, w_key, w_value, query_gain, key_gain, cosine, sine, scale, spread):
    rows, depth = tokens.shape
    hd = query_gain.shape[0]
    qw = w_query.shape[1]
    n_tp = lax.axis_size("tp")
    count = rows * n_tp
    vm = pl.BlockSpec(memory_space=pltpu.VMEM)
    hbm = pl.BlockSpec(memory_space=pl.ANY)
    dma = pltpu.SemaphoreType.DMA
    return pl.pallas_call(
        functools.partial(project_kernel, scale),
        out_shape=(
            jax.ShapeDtypeStruct((spread, count, qw), jnp.bfloat16),
            jax.ShapeDtypeStruct((count, hd), jnp.bfloat16),
            jax.ShapeDtypeStruct((count, hd), jnp.bfloat16),
        ),
        in_specs=[vm, vm, hbm, hbm, hbm, vm, vm, vm, vm],
        out_specs=(hbm, vm, vm),
        scratch_shapes=[
            pltpu.VMEM((n_tp, rows, depth), jnp.bfloat16),
            pltpu.VMEM((depth, qw + 2 * hd), jnp.bfloat16),
            pltpu.VMEM((rows, qw + 2 * hd), jnp.float32),
            pltpu.VMEM((2, n_tp, rows, qw), jnp.bfloat16),
            dma((6,)),
            dma((6,)),
            dma((4,)),
            dma((4,)),
            dma((3, 4)),
            dma((3, 4)),
            dma((4,)),
            dma((4,)),
            dma((3, 4)),
            dma((3, 4)),
            dma((3,)),
            dma((4,)),
        ],
        compiler_params=pltpu.CompilerParams(
            collective_id=0, has_side_effects=True, vmem_limit_bytes=32 * 1024 * 1024
        ),
    )(
        tokens,
        norm_gain[None, :],
        w_query,
        w_key,
        w_value,
        query_gain[None, :],
        key_gain[None, :],
        cosine,
        sine,
    )


def shifted(value, axis, steps):
    count = lax.axis_size(axis)
    pairs = [(source, (source + steps) % count) for source in range(count)]
    return lax.ppermute(value, axis, pairs)


def on_device(
    tokens,
    norm_gain,
    w_query,
    w_key,
    w_value,
    query_gain,
    key_gain,
    w_out,
    cache_keys,
    cache_values,
    cache_plan,
):
    head_dim = query_gain.shape[0]
    q_width = w_query.shape[1]
    q_heads = q_width // head_dim
    requests, spread = cache_plan.shape
    score_scale = head_dim ** (-0.5) * log2e
    device = lax.axis_index("req")
    lengths = jnp.sum(cache_plan, axis=1)
    req_ids = jnp.arange(requests)
    own_length = jnp.sum(jnp.where(req_ids == device, lengths, 0))
    owners = (device - jnp.arange(spread)) % requests
    held = jnp.sum(jnp.where(req_ids[None, :] == owners[:, None], cache_plan.T, 0), axis=1)
    token_rows = tokens.astype(jnp.float32)
    count_new = tokens.shape[0] * lax.axis_size("tp")
    positions = (own_length + jnp.arange(count_new)).astype(jnp.float32)
    freqs = rope_base ** (-(jnp.arange(head_dim // 2).astype(jnp.float32) * 2.0) / head_dim)
    angles = positions[:, None] * freqs[None, :]
    cosine, sine = jnp.cos(angles), jnp.sin(angles)
    arrived, new_keys, new_values = project(
        tokens,
        norm_gain,
        w_query,
        w_key,
        w_value,
        query_gain,
        key_gain,
        jnp.concatenate([cosine, cosine], axis=1),
        jnp.concatenate([-sine, sine], axis=1),
        score_scale,
        spread,
    )
    parts, stats = attn(
        held, arrived, cache_keys, cache_values, new_keys, new_values
    )
    outs = [parts[spread], parts[0]]
    tops = [stats[spread], stats[0]]
    for k in range(1, spread):
        outs.append(shifted(parts[k], "req", -k))
        tops.append(shifted(stats[k], "req", -k))
    tops = jnp.stack(tops)[:, :q_heads]
    shares = jnp.exp2(tops - jnp.max(tops, axis=0, keepdims=True))
    shares = shares / jnp.sum(shares, axis=0, keepdims=True)
    attended = sum(
        out.astype(jnp.float32).reshape(count_new, q_heads, head_dim)
        * shares[i].T[:, :, None]
        for i, out in enumerate(outs)
    )
    attended = attended.reshape(count_new, q_width).astype(jnp.bfloat16)
    summed = lax.psum_scatter(
        jnp.dot(attended, w_out, preferred_element_type=jnp.float32).astype(jnp.bfloat16),
        "tp",
        scatter_dimension=0,
        tiled=True,
    ).astype(jnp.float32)
    return (token_rows + summed).astype(jnp.bfloat16)


def solution(mesh):
    placed = (
        P(("req", "tp"), None),
        P(),
        P(None, "tp"),
        P(None, "tp"),
        P(None, "tp"),
        P(),
        P(),
        P("tp", None),
        P("req", "tp"),
        P("req", "tp"),
        P(),
    )
    return jax.shard_map(
        on_device, mesh=mesh, in_specs=placed, out_specs=P(("req", "tp"), None), check_vma=False
    )
```

```python
import functools
import jax
import jax.numpy as jnp
from jax import lax
from jax.experimental import pallas as pl
from jax.experimental.pallas import tpu as pltpu
from jax.sharding import PartitionSpec as P

norm_eps = 1e-06
rope_base = 1000000.0
log2e = 1.4426950408889634

NEG = -1e30

def softmax_pv(qs, kx, vx, causal=False, order=0):
    outs = []
    def sc(q):
        s = lax.dot_general(q, kx, (((1,), (1,)), ((), ())), preferred_element_type=jnp.float32)
        if causal:
            r = lax.broadcasted_iota(jnp.int32, s.shape, 0); c = lax.broadcasted_iota(jnp.int32, s.shape, 1)
            s = jnp.where(r >= c, s, NEG)
        return s
    ss = [sc(q) for q in qs] if order == 1 else None
    for i, q in enumerate(qs):
        s = ss[i] if ss else sc(q)
        m = jnp.max(s, axis=1, keepdims=True)
        p = jnp.exp2(s - m).astype(jnp.bfloat16)
        oe = jnp.dot(p, vx, preferred_element_type=jnp.float32)
        l = oe[:, 128:]
        outs.append((oe[:, :128] / l, m + jnp.log2(l)))
    return outs

def attn_kernel(order, heads, held_ref, q_ref, k_ref, v_ref, nk_ref, nv_ref, o_ref, st_ref, kx_ref, vx_ref):
    j = pl.program_id(0)
    n = pl.num_programs(0)
    hd = 128
    T = q_ref.shape[1]
    lanes = lax.broadcasted_iota(jnp.int32, (T, hd), 1)

    def emit(outs):
        st = jnp.full((T, hd), NEG, jnp.float32)
        for g, (o, lse) in enumerate(outs):
            o_ref[0, :, g * hd:(g + 1) * hd] = o.astype(jnp.bfloat16)
            st = jnp.where(lanes == g, lse, st)
        turned = jnp.transpose(st)[:8]
        for c in range(T // 64):
            pair = turned[:, c // 2 * 128 : c // 2 * 128 + 128]
            st_ref[0, c] = pltpu.roll(pair, 64, 1) if c % 2 else pair

    def run(length, held):
        rows = lax.broadcasted_iota(jnp.int32, (length, hd), 0)
        ok = rows < held
        kx_ref[:length] = jnp.where(ok, k_ref[:length], jnp.broadcast_to(k_ref[0:1], (length, hd)))
        vx_ref[:length, :hd] = jnp.where(ok, v_ref[:length], jnp.zeros((length, hd), jnp.bfloat16))
        vx_ref[:length, hd:] = jnp.where(ok, 1.0, 0.0).astype(jnp.bfloat16)
        qs = [q_ref[0, :, g * hd:(g + 1) * hd] for g in range(heads)]
        emit(softmax_pv(qs, kx_ref[:length], vx_ref[:length], order=order))

    held = held_ref[jnp.minimum(j, n - 2)]
    full = k_ref.shape[0]
    small = min(full, 512)

    @pl.when(jnp.logical_and(j < n - 1, held > small))
    def _():
        run(full, held)

    @pl.when(jnp.logical_and(j < n - 1, jnp.logical_and(held > 0, held <= small)))
    def _():
        run(small, held)

    @pl.when(jnp.logical_and(j < n - 1, held <= 0))
    def _():
        o_ref[...] = jnp.zeros_like(o_ref)
        st_ref[...] = jnp.full_like(st_ref, NEG)

    @pl.when(j == n - 1)
    def _():
        kx_ref[:T] = nk_ref[...]
        vx_ref[:T, :hd] = nv_ref[...]
        vx_ref[:T, hd:] = jnp.ones((T, hd), jnp.bfloat16)
        qs = [q_ref[0, :, g * hd:(g + 1) * hd] for g in range(heads)]
        emit(softmax_pv(qs, kx_ref[:T], vx_ref[:T], causal=True, order=order))

def attn(held, q, k, v, nk, nv, order=1):
    spread, T, W = q.shape
    hd = k.shape[1]
    cap = k.shape[0] // spread
    return pl.pallas_call(
        functools.partial(attn_kernel, order, W // hd),
        out_shape=(jax.ShapeDtypeStruct((spread + 1, T, W), jnp.bfloat16),
                   jax.ShapeDtypeStruct((spread + 1, T // 64, 8, hd), jnp.float32)),
        grid_spec=pltpu.PrefetchScalarGridSpec(
            num_scalar_prefetch=1, grid=(spread + 1,),
            in_specs=[
                pl.BlockSpec((1, T, W), lambda j, h: (lax.rem(j, spread), 0, 0)),
                pl.BlockSpec((cap, hd), lambda j, h: (jnp.minimum(j, spread - 1), 0)),
                pl.BlockSpec((cap, hd), lambda j, h: (jnp.minimum(j, spread - 1), 0)),
                pl.BlockSpec((T, hd), lambda j, h: (0, 0)),
                pl.BlockSpec((T, hd), lambda j, h: (0, 0)),
            ],
            out_specs=[pl.BlockSpec((1, T, W), lambda j, h: (j, 0, 0)),
                       pl.BlockSpec((1, T // 64, 8, hd), lambda j, h: (j, 0, 0, 0))],
            scratch_shapes=[pltpu.VMEM((cap, hd), jnp.bfloat16), pltpu.VMEM((cap, 2 * hd), jnp.bfloat16)],
        ),
        compiler_params=pltpu.CompilerParams(vmem_limit_bytes=60 * 1024 * 1024),
    )(held, q, k, v, nk, nv)


MESH = pl.DeviceIdType.MESH


def remote(src, dst, send, recv, req, tp):
    return pltpu.make_async_remote_copy(
        src_ref=src,
        dst_ref=dst,
        send_sem=send,
        recv_sem=recv,
        device_id=(req, tp),
        device_id_type=MESH,
    )


def greet(partners):
    barrier = pltpu.get_barrier_semaphore()
    for where in partners:
        pl.semaphore_signal(barrier, inc=1, device_id=where, device_id_type=MESH)
    pl.semaphore_wait(barrier, len(partners))


def spots():
    req, tp = lax.axis_index("req"), lax.axis_index("tp")
    n_tp = lax.axis_size("tp")
    core = lax.rem(req, 2)
    z = lax.rem(req // 2, 4)
    plane = req - 2 * z - core
    n_req = lax.axis_size("req")
    return req, tp, n_tp, n_req, core, z, plane


def project_kernel(
    score_scale,
    tok_ref,
    gain_ref,
    wq_ref,
    wk_ref,
    wv_ref,
    qg_ref,
    kg_ref,
    cos_ref,
    sin_ref,
    all_ref,
    nk_ref,
    nv_ref,
    xs,
    w,
    acc,
    qbuf,
    ag_send,
    ag_recv,
    y_send,
    y_recv,
    z_send,
    z_recv,
    d_send,
    d_recv,
    f_send,
    f_recv,
    w_sem,
    own_sem,
):
    req, tp, n_tp, n_req, core, z, plane = spots()
    rows = tok_ref.shape[0]
    half = rows // 2
    hd = qg_ref.shape[1]
    qw = wq_ref.shape[1]
    heads = qw // hd
    depth = tok_ref.shape[1]
    right, left = lax.rem(tp + 1, n_tp), lax.rem(tp + n_tp - 1, n_tp)
    y_next, y_prev = lax.rem(req + 8, n_req), lax.rem(req + n_req - 8, n_req)
    mate = req + 1 - 2 * core

    def z_peer(dz):
        return plane + 2 * lax.rem(z + dz, 4) + core

    w_copies = [
        pltpu.make_async_copy(wq_ref, w.at[:, :qw], w_sem.at[0]),
        pltpu.make_async_copy(wk_ref, w.at[:, qw : qw + hd], w_sem.at[1]),
        pltpu.make_async_copy(wv_ref, w.at[:, qw + hd :], w_sem.at[2]),
    ]
    for copy in w_copies:
        copy.start()
    greet(
        [(req, right), (req, left), (y_next, tp), (y_prev, tp), (mate, tp)]
        + [(z_peer(dz), tp) for dz in (1, 2, 3)]
    )
    tok = tok_ref[...].astype(jnp.float32)
    scale = lax.rsqrt(jnp.mean(tok * tok, axis=-1, keepdims=True) + norm_eps)
    xs[0] = (tok * scale * gain_ref[...].astype(jnp.float32)).astype(jnp.bfloat16)

    low, high = slice(0, half), slice(half, rows)

    def ag(index, slot_from, slot_to, part, target):
        return remote(
            xs.at[slot_from, part],
            xs.at[slot_to, part],
            ag_send.at[index],
            ag_recv.at[index],
            req,
            target,
        )

    ag_copies = [
        ag(0, 0, 1, low, right),
        ag(1, 0, 3, high, left),
        ag(2, 0, 1, high, right),
        ag(3, 0, 3, low, left),
        ag(4, 1, 2, low, right),
        ag(5, 3, 2, high, left),
    ]
    for copy in ag_copies[:4]:
        copy.start()
    for copy in w_copies:
        copy.wait()

    def first_row(s):
        return pl.multiple_of(lax.rem(tp + n_tp - s, n_tp) * rows, rows)

    def slot_rows(k, s):
        return all_ref.at[k, pl.ds(first_row(s), rows), :]

    def y_copy(s):
        return remote(qbuf.at[0, s], qbuf.at[1, s], y_send.at[s], y_recv.at[s], y_next, tp)

    def z_copy(dz, s):
        return remote(
            qbuf.at[(z + dz) // 4, s],
            slot_rows(2 * dz, s),
            z_send.at[dz - 1, s],
            z_recv.at[dz - 1, s],
            z_peer(dz),
            tp,
        )

    def d_copy(s):
        return remote(
            qbuf.at[core, s], slot_rows(1 + 6 * core, s), d_send.at[s], d_recv.at[s], mate, tp
        )

    def f_copy(dz, s):
        return remote(
            slot_rows(2 * dz, s),
            slot_rows(2 * dz + 1 - 2 * core, s),
            f_send.at[dz - 1, s],
            f_recv.at[dz - 1, s],
            mate,
            tp,
        )

    def own_copy(s):
        return pltpu.make_async_copy(qbuf.at[0, s], slot_rows(0, s), own_sem.at[s])

    def stage(s):
        acc[...] = jnp.zeros_like(acc)
        width = depth // 5

        def block(b, carry):
            at = pl.ds(pl.multiple_of(b * width, width), width)
            acc[...] += jnp.dot(xs[s, :, at], w[at, :], preferred_element_type=jnp.float32)
            return carry

        lax.fori_loop(0, 5, block, 0)
        here = pl.ds(first_row(s), rows)
        cosine, sine = cos_ref[here, :], sin_ref[here, :]

        def turned(at, gain):
            head = acc[:, at : at + hd]
            head = head * lax.rsqrt(jnp.mean(head * head, axis=-1, keepdims=True) + norm_eps) * gain
            return head * cosine + pltpu.roll(head, hd // 2, 1) * sine

        q_gain = qg_ref[...].astype(jnp.float32) * score_scale
        for h in range(heads):
            qbuf[0, s, :, h * hd : (h + 1) * hd] = turned(h * hd, q_gain).astype(jnp.bfloat16)
        nk_ref[here, :] = turned(qw, kg_ref[...].astype(jnp.float32)).astype(jnp.bfloat16)
        nv_ref[here, :] = acc[:, qw + hd :].astype(jnp.bfloat16)
        y_copy(s).start()
        for dz in (1, 2, 3):

            @pl.when(z + dz < 4)
            def _():
                z_copy(dz, s).start()

        @pl.when(core == 0)
        def _():
            d_copy(s).start()

        own_copy(s).start()

    def relay(s):
        y_copy(s).wait_recv()
        for dz in (1, 2, 3):

            @pl.when(z + dz >= 4)
            def _():
                z_copy(dz, s).start()

        @pl.when(core == 1)
        def _():
            d_copy(s).start()

    def pass_on(s):
        for dz in (1, 2, 3):
            z_copy(dz, s).wait_recv()
            f_copy(dz, s).start()

    stage(0)
    ag_copies[0].wait_recv()
    ag_copies[4].start()
    ag_copies[1].wait_recv()
    ag_copies[5].start()
    relay(0)
    ag_copies[2].wait_recv()
    stage(1)
    ag_copies[3].wait_recv()
    pass_on(0)
    stage(3)
    relay(1)
    relay(3)
    ag_copies[4].wait_recv()
    ag_copies[5].wait_recv()
    stage(2)
    pass_on(1)
    pass_on(3)
    relay(2)
    pass_on(2)
    for s in range(4):
        d_copy(s).wait_recv()
        for dz in (1, 2, 3):
            f_copy(dz, s).wait_recv()
    for copy in ag_copies:
        copy.wait_send()
    for s in range(4):
        own_copy(s).wait()
        y_copy(s).wait_send()
        d_copy(s).wait_send()
        for dz in (1, 2, 3):
            z_copy(dz, s).wait_send()
            f_copy(dz, s).wait_send()


def project(tokens, norm_gain, w_query, w_key, w_value, query_gain, key_gain, cosine, sine, scale, spread):
    rows, depth = tokens.shape
    hd = query_gain.shape[0]
    qw = w_query.shape[1]
    n_tp = lax.axis_size("tp")
    count = rows * n_tp
    vm = pl.BlockSpec(memory_space=pltpu.VMEM)
    hbm = pl.BlockSpec(memory_space=pl.ANY)
    dma = pltpu.SemaphoreType.DMA
    return pl.pallas_call(
        functools.partial(project_kernel, scale),
        out_shape=(
            jax.ShapeDtypeStruct((spread, count, qw), jnp.bfloat16),
            jax.ShapeDtypeStruct((count, hd), jnp.bfloat16),
            jax.ShapeDtypeStruct((count, hd), jnp.bfloat16),
        ),
        in_specs=[vm, vm, hbm, hbm, hbm, vm, vm, vm, vm],
        out_specs=(hbm, vm, vm),
        scratch_shapes=[
            pltpu.VMEM((n_tp, rows, depth), jnp.bfloat16),
            pltpu.VMEM((depth, qw + 2 * hd), jnp.bfloat16),
            pltpu.VMEM((rows, qw + 2 * hd), jnp.float32),
            pltpu.VMEM((2, n_tp, rows, qw), jnp.bfloat16),
            dma((6,)),
            dma((6,)),
            dma((4,)),
            dma((4,)),
            dma((3, 4)),
            dma((3, 4)),
            dma((4,)),
            dma((4,)),
            dma((3, 4)),
            dma((3, 4)),
            dma((3,)),
            dma((4,)),
        ],
        compiler_params=pltpu.CompilerParams(
            collective_id=0, has_side_effects=True, vmem_limit_bytes=32 * 1024 * 1024
        ),
    )(
        tokens,
        norm_gain[None, :],
        w_query,
        w_key,
        w_value,
        query_gain[None, :],
        key_gain[None, :],
        cosine,
        sine,
    )


def finish_kernel(
    tok_ref,
    parts_ref,
    stat_ref,
    wo_ref,
    out_ref,
    pbuf,
    w,
    mbuf,
    mst,
    dbuf,
    dst,
    sbuf,
    sst,
    rbuf,
    rst,
    psend,
    pre,
    full,
    total,
    m_send,
    m_recv,
    ms_send,
    ms_recv,
    d_send,
    d_recv,
    ds_send,
    ds_recv,
    r_send,
    r_recv,
    rs_send,
    rs_recv,
    x_send,
    x_recv,
    load_sem,
):
    req, tp, n_tp, n_req, core, z, plane = spots()
    rows, depth = tok_ref.shape
    half = rows // 2
    qw = wo_ref.shape[0]
    hd = stat_ref.shape[3]
    heads = qw // hd
    last = parts_ref.shape[0] - 1
    right, left = lax.rem(tp + 1, n_tp), lax.rem(tp + n_tp - 1, n_tp)
    mate = req + 1 - 2 * core
    lone = 7 - 6 * core

    def ahead(steps):
        return lax.rem(req + n_req + steps, n_req)

    load_parts = pltpu.make_async_copy(parts_ref, pbuf, load_sem.at[0])
    load_w = pltpu.make_async_copy(wo_ref, w, load_sem.at[1])
    load_parts.start()
    load_w.start()
    greet(
        [(req, right), (req, left), (mate, tp), (ahead(14 * core - 7), tp)]
        + [(ahead(steps), tp) for steps in (2, 4, 6, -2, -4, -6)]
    )

    def chunk(off):
        return lax.rem(tp + off, n_tp)

    def here(off):
        return pl.ds(pl.multiple_of(chunk(off) * rows, rows), rows)

    def m_copy(dz, off):
        return remote(
            parts_ref.at[2 * dz - 1 + 2 * core, here(off), :],
            mbuf.at[dz - 1, off],
            m_send.at[dz - 1, off],
            m_recv.at[dz - 1, off],
            mate,
            tp,
        )

    def ms_copy(dz):
        return remote(
            stat_ref.at[2 * dz - 1 + 2 * core],
            mst.at[dz - 1],
            ms_send.at[dz - 1],
            ms_recv.at[dz - 1],
            mate,
            tp,
        )

    def d_copy(off):
        return remote(
            parts_ref.at[lone, here(off), :],
            dbuf.at[off],
            d_send.at[off],
            d_recv.at[off],
            ahead(-lone),
            tp,
        )

    def ds_copy():
        return remote(
            stat_ref.at[lone], dst, ds_send.at[0], ds_recv.at[0], ahead(-lone), tp
        )

    def r_copy(dz, off):
        return remote(
            sbuf.at[dz - 1, off],
            rbuf.at[dz - 1, off],
            r_send.at[dz - 1, off],
            r_recv.at[dz - 1, off],
            ahead(-2 * dz),
            tp,
        )

    def rs_copy(dz, off):
        return remote(
            sst.at[dz - 1, off],
            rst.at[dz - 1, off],
            rs_send.at[dz - 1, off],
            rs_recv.at[dz - 1, off],
            ahead(-2 * dz),
            tp,
        )

    low, high = slice(0, half), slice(half, rows)

    def x_copy(index, src, target_ref, target):
        return remote(src, target_ref, x_send.at[index], x_recv.at[index], req, target)

    x_copies = [
        x_copy(0, psend.at[1, low], pre.at[0], right),
        x_copy(1, psend.at[1, high], pre.at[1], left),
        x_copy(2, psend.at[0, high], full.at[0, high], right),
        x_copy(3, psend.at[0, low], full.at[0, low], right),
        x_copy(4, psend.at[2, low], full.at[1, low], left),
        x_copy(5, psend.at[2, high], full.at[1, high], left),
    ]

    order = (2, 1, 3, 0)
    dzs = (1, 2, 3)
    for dz in dzs:
        ms_copy(dz).start()
    ds_copy().start()
    for off in order:
        for dz in dzs:
            m_copy(dz, off).start()
        d_copy(off).start()
    load_parts.wait()
    load_w.wait()

    def columns(pieces):
        flat = jnp.concatenate(
            pieces + [jnp.zeros((128 - 8 * len(pieces), hd), jnp.float32)], axis=0
        )
        return jnp.transpose(flat)[:rows]

    def widen(value):
        return value.astype(jnp.float32)

    def pair_up(off):
        if off == order[0]:
            for dz in dzs:
                ms_copy(dz).wait_recv()
        shares = []
        for dz in dzs:
            mine, other = stat_ref[2 * dz, chunk(off)], mst[dz - 1, chunk(off)]
            top = jnp.maximum(mine, other)
            mine, other = jnp.exp2(mine - top), jnp.exp2(other - top)
            mass = mine + other
            sst[dz - 1, off] = top + jnp.log2(mass)
            shares += [mine / mass, other / mass]
        table = columns(shares)
        for dz in dzs:
            m_copy(dz, off).wait_recv()
            for h in range(heads):
                at = slice(h * hd, (h + 1) * hd)
                i, j = 16 * (dz - 1) + h, 16 * (dz - 1) + 8 + h
                both = widen(pbuf[2 * dz, here(off), at]) * table[:, i : i + 1]
                both += widen(mbuf[dz - 1, off, :, at]) * table[:, j : j + 1]
                sbuf[dz - 1, off, :, at] = both.astype(jnp.bfloat16)
            rs_copy(dz, off).start()
            r_copy(dz, off).start()

    def merged(off):
        if off == order[0]:
            ds_copy().wait_recv()
        d_copy(off).wait_recv()
        for dz in dzs:
            rs_copy(dz, off).wait_recv()
            r_copy(dz, off).wait_recv()
        tops = [stat_ref[last, chunk(off)], stat_ref[0, chunk(off)], dst[chunk(off)]]
        tops += [rst[dz - 1, off] for dz in dzs]
        top = functools.reduce(jnp.maximum, tops)
        masses = [jnp.exp2(one - top) for one in tops]
        mass = functools.reduce(jnp.add, masses)
        table = columns([one / mass for one in masses])
        heads_out = []
        for h in range(heads):
            at = slice(h * hd, (h + 1) * hd)
            sources = [pbuf[last, here(off), at], pbuf[0, here(off), at], dbuf[off, :, at]]
            sources += [rbuf[dz - 1, off, :, at] for dz in dzs]
            value = jnp.zeros((rows, hd), jnp.float32)
            for n, source in enumerate(sources):
                i = 8 * n + h
                value += widen(source) * table[:, i : i + 1]
            heads_out.append(value.astype(jnp.bfloat16))
        return jnp.concatenate(heads_out, axis=1)

    width = depth // 5

    def outward(off, store):
        attended = merged(off)

        def tile(b, carry):
            at = pl.ds(pl.multiple_of(b * width, width), width)
            store(at, jnp.dot(attended, w[:, at], preferred_element_type=jnp.float32))
            return carry

        lax.fori_loop(0, 5, tile, 0)

    def to_send(off):
        def store(at, value):
            psend[off - 1, :, at] = value.astype(jnp.bfloat16)

        outward(off, store)

    def join(off, part, slot):
        psend[off - 1, part] = (widen(psend[off - 1, part]) + widen(pre[slot])).astype(
            jnp.bfloat16
        )

    pair_up(2)
    pair_up(1)
    to_send(2)
    x_copies[0].start()
    x_copies[1].start()
    pair_up(3)
    to_send(1)
    x_copies[2].start()
    x_copies[0].wait_recv()
    join(1, low, 0)
    x_copies[3].start()
    pair_up(0)
    to_send(3)
    x_copies[4].start()
    x_copies[1].wait_recv()
    join(3, high, 1)
    x_copies[5].start()

    def keep(at, value):
        total[:, at] = widen(tok_ref[:, at]) + widen(value.astype(jnp.bfloat16))

    outward(0, keep)
    for n in (2, 3, 4, 5):
        x_copies[n].wait_recv()
    out_ref[...] = (total[...] + widen(full[0]) + widen(full[1])).astype(jnp.bfloat16)
    for copy in x_copies:
        copy.wait_send()
    ds_copy().wait_send()
    for dz in dzs:
        ms_copy(dz).wait_send()
    for off in order:
        d_copy(off).wait_send()
        for dz in dzs:
            m_copy(dz, off).wait_send()
            r_copy(dz, off).wait_send()
            rs_copy(dz, off).wait_send()


def finish(tokens, parts, stats, w_out):
    rows, depth = tokens.shape
    qw = w_out.shape[0]
    hd = stats.shape[3]
    n_tp = lax.axis_size("tp")
    vm = pl.BlockSpec(memory_space=pltpu.VMEM)
    hbm = pl.BlockSpec(memory_space=pl.ANY)
    dma = pltpu.SemaphoreType.DMA
    block = (rows, qw)
    stat = (8, hd)
    return pl.pallas_call(
        finish_kernel,
        out_shape=jax.ShapeDtypeStruct((rows, depth), jnp.bfloat16),
        in_specs=[vm, hbm, vm, hbm],
        out_specs=vm,
        scratch_shapes=[
            pltpu.VMEM(parts.shape, jnp.bfloat16),
            pltpu.VMEM(w_out.shape, jnp.bfloat16),
            pltpu.VMEM((3, n_tp) + block, jnp.bfloat16),
            pltpu.VMEM((3, n_tp) + stat, jnp.float32),
            pltpu.VMEM((n_tp,) + block, jnp.bfloat16),
            pltpu.VMEM((n_tp,) + stat, jnp.float32),
            pltpu.VMEM((3, n_tp) + block, jnp.bfloat16),
            pltpu.VMEM((3, n_tp) + stat, jnp.float32),
            pltpu.VMEM((3, n_tp) + block, jnp.bfloat16),
            pltpu.VMEM((3, n_tp) + stat, jnp.float32),
            pltpu.VMEM((3, rows, depth), jnp.bfloat16),
            pltpu.VMEM((2, rows // 2, depth), jnp.bfloat16),
            pltpu.VMEM((2, rows, depth), jnp.bfloat16),
            pltpu.VMEM((rows, depth), jnp.float32),
            dma((3, 4)),
            dma((3, 4)),
            dma((3,)),
            dma((3,)),
            dma((4,)),
            dma((4,)),
            dma((1,)),
            dma((1,)),
            dma((3, 4)),
            dma((3, 4)),
            dma((3, 4)),
            dma((3, 4)),
            dma((6,)),
            dma((6,)),
            dma((2,)),
        ],
        compiler_params=pltpu.CompilerParams(
            collective_id=1, has_side_effects=True, vmem_limit_bytes=40 * 1024 * 1024
        ),
    )(tokens, parts, stats, w_out)


def on_device(
    tokens,
    norm_gain,
    w_query,
    w_key,
    w_value,
    query_gain,
    key_gain,
    w_out,
    cache_keys,
    cache_values,
    cache_plan,
):
    head_dim = query_gain.shape[0]
    q_width = w_query.shape[1]
    q_heads = q_width // head_dim
    requests, spread = cache_plan.shape
    score_scale = head_dim ** (-0.5) * log2e
    device = lax.axis_index("req")
    lengths = jnp.sum(cache_plan, axis=1)
    req_ids = jnp.arange(requests)
    own_length = jnp.sum(jnp.where(req_ids == device, lengths, 0))
    owners = (device - jnp.arange(spread)) % requests
    held = jnp.sum(jnp.where(req_ids[None, :] == owners[:, None], cache_plan.T, 0), axis=1)
    count_new = tokens.shape[0] * lax.axis_size("tp")
    positions = (own_length + jnp.arange(count_new)).astype(jnp.float32)
    freqs = rope_base ** (-(jnp.arange(head_dim // 2).astype(jnp.float32) * 2.0) / head_dim)
    angles = positions[:, None] * freqs[None, :]
    cosine, sine = jnp.cos(angles), jnp.sin(angles)
    arrived, new_keys, new_values = project(
        tokens,
        norm_gain,
        w_query,
        w_key,
        w_value,
        query_gain,
        key_gain,
        jnp.concatenate([cosine, cosine], axis=1),
        jnp.concatenate([-sine, sine], axis=1),
        score_scale,
        spread,
    )
    parts, stats = attn(
        held, arrived, cache_keys, cache_values, new_keys, new_values
    )
    return finish(tokens, parts, stats, w_out)


def solution(mesh):
    placed = (
        P(("req", "tp"), None),
        P(),
        P(None, "tp"),
        P(None, "tp"),
        P(None, "tp"),
        P(),
        P(),
        P("tp", None),
        P("req", "tp"),
        P("req", "tp"),
        P(),
    )
    return jax.shard_map(
        on_device, mesh=mesh, in_specs=placed, out_specs=P(("req", "tp"), None), check_vma=False
    )
```

```python
import functools
import jax
import jax.numpy as jnp
import numpy as np
from jax import lax
from jax.experimental import pallas as pl
from jax.experimental.pallas import tpu as pltpu
from jax.sharding import PartitionSpec as P

norm_eps = 1e-06
rope_base = 1000000.0
log2e = 1.4426950408889634
NEG = -1e30
MESH = pl.DeviceIdType.MESH
coarse_rows = 136


def widen(value):
    return value.astype(jnp.float32)


def remote(src, dst, send, recv, req, tp):
    return pltpu.make_async_remote_copy(
        src_ref=src,
        dst_ref=dst,
        send_sem=send,
        recv_sem=recv,
        device_id=(req, tp),
        device_id_type=MESH,
    )


def kernel(
    score_scale,
    plan_ref,
    vec_ref,
    tab_hbm,
    tok_hbm,
    wq_hbm,
    wk_hbm,
    wv_hbm,
    wo_hbm,
    k_hbm,
    v_hbm,
    out_ref,
    tab,
    tok,
    xs,
    w,
    wo,
    acc,
    kx,
    vx,
    nk,
    nv,
    qs,
    qprev,
    obuf,
    onew,
    stat,
    mbuf,
    mst,
    dbuf,
    dst,
    sbuf,
    sst,
    rbuf,
    rst,
    psend,
    pre,
    full,
    total,
    load_sem,
    ag_send,
    ag_recv,
    y_send,
    y_recv,
    z_send,
    z_recv,
    p_send,
    p_recv,
    f_send,
    f_recv,
    m_send,
    m_recv,
    ms_send,
    ms_recv,
    d_send,
    d_recv,
    ds_send,
    ds_recv,
    r_send,
    r_recv,
    rs_send,
    rs_recv,
    x_send,
    x_recv,
):
    req, tp = lax.axis_index("req"), lax.axis_index("tp")
    n_req, n_tp = lax.axis_size("req"), lax.axis_size("tp")
    core = lax.rem(req, 2)
    z = lax.rem(req // 2, 4)
    plane = req - 2 * z - core
    rows, depth = tok.shape
    half = rows // 2
    spread = plan_ref.shape[1]
    cap = kx.shape[0] // spread
    hd = kx.shape[1]
    qw = wo.shape[0]
    heads = qw // hd
    tall = heads * rows
    right, left = lax.rem(tp + 1, n_tp), lax.rem(tp + n_tp - 1, n_tp)
    mate = req + 1 - 2 * core
    lone = 7 - 6 * core
    dzs = (1, 2, 3)
    low, high = slice(0, half), slice(half, rows)

    def ahead(steps):
        return lax.rem(req + n_req + steps, n_req)

    def z_peer(dz):
        return plane + 2 * lax.rem(z + dz, 4) + core

    def load(index, src, target):
        return pltpu.make_async_copy(src, target, load_sem.at[index])

    load_tok = load(0, tok_hbm, tok)
    load_w = [
        load(1, wq_hbm, w.at[:, :qw]),
        load(2, wk_hbm, w.at[:, qw : qw + hd]),
        load(3, wv_hbm, w.at[:, qw + hd :]),
    ]
    load_tab = load(4, tab_hbm, tab)
    load_kv = [load(5, k_hbm, kx), load(6, v_hbm, vx.at[:, :hd])]
    load_wo = load(7, wo_hbm, wo)
    load_tok.start()
    for copy in load_w:
        copy.start()
    load_tab.start()

    barrier = pltpu.get_barrier_semaphore()
    partners = [(req, right), (req, left), (mate, tp), (ahead(14 * core - 7), tp)]
    partners += [(ahead(steps), tp) for steps in (8, -8, 2, 4, 6, -2, -4, -6)]
    partners += [(z_peer(dz), tp) for dz in dzs]
    for where in partners:
        pl.semaphore_signal(barrier, inc=1, device_id=where, device_id_type=MESH)

    load_tok.wait()
    value = widen(tok[...])
    scale = lax.rsqrt(jnp.mean(value * value, axis=-1, keepdims=True) + norm_eps)
    xs[0] = (value * scale * vec_ref[:, :depth]).astype(jnp.bfloat16)
    q_gain = vec_ref[:, depth : depth + hd] * score_scale
    k_gain = vec_ref[:, depth + hd :]
    pl.semaphore_wait(barrier, len(partners))

    def ag(index, at_from, at_to, part, target):
        return remote(
            xs.at[at_from, part],
            xs.at[at_to, part],
            ag_send.at[index],
            ag_recv.at[index],
            req,
            target,
        )

    ag_copies = [
        ag(0, 0, 1, low, right),
        ag(1, 0, 2, high, left),
        ag(2, 0, 1, high, right),
        ag(3, 0, 2, low, left),
        ag(4, 1, 3, low, right),
        ag(5, 2, 3, high, left),
    ]
    for copy in ag_copies[:4]:
        copy.start()

    def first_row(s):
        return pl.multiple_of(lax.rem(tp + n_tp - s, n_tp) * rows, rows)

    def y_copy(s):
        return remote(qs.at[0, s], qprev.at[s], y_send.at[s], y_recv.at[s], ahead(8), tp)

    def z_copy(dz, s, src):
        return remote(
            src, qs.at[2 * dz, s], z_send.at[dz - 1, s], z_recv.at[dz - 1, s], z_peer(dz), tp
        )

    def p_copy(s, src):
        return remote(src, qs.at[1 + 6 * core, s], p_send.at[s], p_recv.at[s], mate, tp)

    def f_copy(dz, s):
        return remote(
            qs.at[2 * dz, s],
            qs.at[2 * dz + 1 - 2 * core, s],
            f_send.at[dz - 1, s],
            f_recv.at[dz - 1, s],
            mate,
            tp,
        )

    length = plan_ref[req, 0]
    for k in range(1, spread):
        length += plan_ref[req, k]
    coarse = length // 128
    fine = coarse_rows + length - coarse * 128

    def stage(blocks, at, n):
        width = depth // 5
        acc[: n * rows] = jnp.zeros((n * rows, acc.shape[1]), jnp.float32)

        def block(b, carry):
            cols = pl.ds(pl.multiple_of(b * width, width), width)
            left_side = xs[at : at + n, :, cols].reshape(n * rows, width)
            acc[: n * rows] += jnp.dot(
                left_side, w[cols, :], preferred_element_type=jnp.float32
            )
            return carry

        lax.fori_loop(0, 5, block, 0)
        c_a, s_a = tab[0, pl.ds(coarse, 1), :], tab[1, pl.ds(coarse, 1), :]
        c_b, s_b = tab[0, pl.ds(fine, 1), :], tab[1, pl.ds(fine, 1), :]
        c_l, s_l = c_a * c_b - s_a * s_b, s_a * c_b + c_a * s_b
        for i, s in enumerate(blocks):
            here = pl.ds(first_row(s), rows)
            there = pl.ds(pl.multiple_of(coarse_rows + first_row(s), 8), rows)
            c_t, s_t = tab[0, there, :], tab[1, there, :]
            cosine, sine = c_t * c_l - s_t * s_l, s_t * c_l + c_t * s_l

            def turned(col, gain):
                head = acc[i * rows : (i + 1) * rows, col : col + hd]
                mean = jnp.mean(head * head, axis=-1, keepdims=True)
                head = head * lax.rsqrt(mean + norm_eps) * gain
                return (head * cosine + pltpu.roll(head, hd // 2, 1) * sine).astype(
                    jnp.bfloat16
                )

            for h in range(heads):
                qs[0, s, h * rows : (h + 1) * rows] = turned(h * hd, q_gain)
            nk[here, :] = turned(qw, k_gain)
            nv[here, :hd] = acc[i * rows : (i + 1) * rows, qw + hd :].astype(jnp.bfloat16)
            y_copy(s).start()
            for dz in dzs:

                @pl.when(z + dz < 4)
                def _():
                    z_copy(dz, s, qs.at[0, s]).start()

            @pl.when(core == 0)
            def _():
                p_copy(s, qs.at[0, s]).start()

    def relay(s):
        y_copy(s).wait_recv()
        for dz in dzs:

            @pl.when(z + dz >= 4)
            def _():
                z_copy(dz, s, qprev.at[s]).start()

        @pl.when(core == 1)
        def _():
            p_copy(s, qprev.at[s]).start()

    def pass_on(s):
        for dz in dzs:
            z_copy(dz, s, qprev.at[s]).wait_recv()
            f_copy(dz, s).start()

    def arrive(s):
        p_copy(s, qprev.at[s]).wait_recv()
        for dz in dzs:
            f_copy(dz, s).wait_recv()

    def softmax(scores, values):
        top = jnp.max(scores, axis=1, keepdims=True)
        weights = jnp.exp2(scores - top).astype(jnp.bfloat16)
        both = jnp.dot(weights, values, preferred_element_type=jnp.float32)
        return both[:, :hd], both[:, hd:], top

    def dot_t(a, b):
        return lax.dot_general(a, b, (((1,), (1,)), ((), ())), preferred_element_type=jnp.float32)

    lanes = lax.broadcasted_iota(jnp.int32, (rows, hd), 1)

    def settle(parts):
        summed = jnp.concatenate([one[0] for one in parts], axis=0)
        mass = jnp.concatenate([one[1] for one in parts], axis=0)
        top = jnp.concatenate([one[2] for one in parts], axis=0)
        some = mass > 0
        value = jnp.where(some, summed / mass, 0.0).astype(jnp.bfloat16)
        level = jnp.where(some, top + jnp.log2(mass), NEG)
        table = jnp.full((rows, hd), NEG, jnp.float32)
        for h in range(heads):
            table = jnp.where(lanes == h, level[h * rows : (h + 1) * rows], table)
        table = jnp.concatenate([table, jnp.zeros_like(table)], axis=0)
        return value, jnp.transpose(table)[:8]

    def attend(blocks, first, last, unroll):
        sub = tall // 2

        def piece(k, carry):
            keys = kx[pl.ds(pl.multiple_of(k * cap, cap), cap), :]
            values = vx[pl.ds(pl.multiple_of(k * cap, cap), cap), :]
            scores = [
                dot_t(qs[k, s, n * sub : (n + 1) * sub], keys) for s in blocks for n in range(2)
            ]
            done = [softmax(one, values) for one in scores]
            for i, s in enumerate(blocks):
                obuf[k, s], stat[k, s] = settle(done[2 * i : 2 * i + 2])
            return carry

        lax.fori_loop(first, last, piece, 0, unroll=unroll)

    def attend_new(s):
        scores = dot_t(qs[0, s], nk[...])
        row = lax.broadcasted_iota(jnp.int32, scores.shape, 0)
        row = first_row(s) + jnp.bitwise_and(row, rows - 1)
        col = lax.broadcasted_iota(jnp.int32, scores.shape, 1)
        scores = jnp.where(row >= col, scores, NEG)
        onew[s], stat[spread, s] = settle([softmax(scores, nv[...])])

    def prepare():
        def piece(k, carry):
            at = pl.ds(pl.multiple_of(k * cap, cap), cap)
            count = plan_ref[lax.rem(req + n_req - k, n_req), k]
            row = lax.broadcasted_iota(jnp.int32, (cap, hd), 0)
            ok = row < count
            keys = kx[at, :]
            kx[at, :] = jnp.where(ok, keys, jnp.broadcast_to(keys[0:1], keys.shape))
            vx[at, :hd] = jnp.where(ok, vx[at, :hd], jnp.zeros((cap, hd), jnp.bfloat16))
            vx[at, hd:] = jnp.where(ok, 1.0, 0.0).astype(jnp.bfloat16)
            return carry

        lax.fori_loop(0, spread, piece, 0)
        nv[:, hd:] = jnp.ones((nv.shape[0], hd), jnp.bfloat16)

    def m_copy(dz, s):
        return remote(
            obuf.at[2 * dz - 1 + 2 * core, s],
            mbuf.at[dz - 1, s],
            m_send.at[dz - 1, s],
            m_recv.at[dz - 1, s],
            mate,
            tp,
        )

    def ms_copy(dz, s):
        return remote(
            stat.at[2 * dz - 1 + 2 * core, s],
            mst.at[dz - 1, s],
            ms_send.at[dz - 1, s],
            ms_recv.at[dz - 1, s],
            mate,
            tp,
        )

    def d_copy(s):
        return remote(obuf.at[lone, s], dbuf.at[s], d_send.at[s], d_recv.at[s], ahead(-lone), tp)

    def ds_copy(s):
        return remote(stat.at[lone, s], dst.at[s], ds_send.at[s], ds_recv.at[s], ahead(-lone), tp)

    def r_copy(dz, s):
        return remote(
            sbuf.at[dz - 1, s],
            rbuf.at[dz - 1, s],
            r_send.at[dz - 1, s],
            r_recv.at[dz - 1, s],
            ahead(-2 * dz),
            tp,
        )

    def rs_copy(dz, s):
        return remote(
            sst.at[dz - 1, s],
            rst.at[dz - 1, s],
            rs_send.at[dz - 1, s],
            rs_recv.at[dz - 1, s],
            ahead(-2 * dz),
            tp,
        )

    def exchange(s):
        for dz in dzs:
            ms_copy(dz, s).start()
            m_copy(dz, s).start()
        ds_copy(s).start()
        d_copy(s).start()

    def columns(pieces):
        pad = jnp.zeros((128 - 8 * len(pieces), hd), jnp.float32)
        return jnp.transpose(jnp.concatenate(pieces + [pad], axis=0))[:rows]

    def pair_up(s):
        for dz in dzs:
            ms_copy(dz, s).wait_recv()
        shares = []
        for dz in dzs:
            mine, other = stat[2 * dz, s], mst[dz - 1, s]
            top = jnp.maximum(mine, other)
            mine, other = jnp.exp2(mine - top), jnp.exp2(other - top)
            mass = mine + other
            sst[dz - 1, s] = top + jnp.log2(mass)
            shares += [mine / mass, other / mass]
        table = columns(shares)
        for dz in dzs:
            m_copy(dz, s).wait_recv()
            for h in range(heads):
                at = slice(h * rows, (h + 1) * rows)
                i, j = 16 * (dz - 1) + h, 16 * (dz - 1) + 8 + h
                both = widen(obuf[2 * dz, s, at]) * table[:, i : i + 1]
                both += widen(mbuf[dz - 1, s, at]) * table[:, j : j + 1]
                sbuf[dz - 1, s, at] = both.astype(jnp.bfloat16)
            rs_copy(dz, s).start()
            r_copy(dz, s).start()

    def merged(s):
        ds_copy(s).wait_recv()
        d_copy(s).wait_recv()
        for dz in dzs:
            rs_copy(dz, s).wait_recv()
            r_copy(dz, s).wait_recv()
        tops = [stat[spread, s], stat[0, s], dst[s]] + [rst[dz - 1, s] for dz in dzs]
        top = functools.reduce(jnp.maximum, tops)
        masses = [jnp.exp2(one - top) for one in tops]
        mass = functools.reduce(jnp.add, masses)
        table = columns([one / mass for one in masses])
        heads_out = []
        for h in range(heads):
            at = slice(h * rows, (h + 1) * rows)
            sources = [onew[s, at], obuf[0, s, at], dbuf[s, at]]
            sources += [rbuf[dz - 1, s, at] for dz in dzs]
            value = jnp.zeros((rows, hd), jnp.float32)
            for n, source in enumerate(sources):
                i = 8 * n + h
                value += widen(source) * table[:, i : i + 1]
            heads_out.append(value.astype(jnp.bfloat16))
        return jnp.concatenate(heads_out, axis=1)

    def outward(s, store):
        width = depth // 5
        attended = merged(s)

        def tile(b, carry):
            at = pl.ds(pl.multiple_of(b * width, width), width)
            store(at, jnp.dot(attended, wo[:, at], preferred_element_type=jnp.float32))
            return carry

        lax.fori_loop(0, 5, tile, 0)

    def to_send(s):
        def store(at, value):
            psend[s - 1, :, at] = value.astype(jnp.bfloat16)

        outward(s, store)

    def x_copy(index, src, target_ref, target):
        return remote(src, target_ref, x_send.at[index], x_recv.at[index], req, target)

    halves = [slice(0, depth // 2), slice(depth // 2, depth)]
    x_far_low = [
        x_copy(i, psend.at[1, low, at], pre.at[0, :, at], right) for i, at in enumerate(halves)
    ]
    x_far_high = [
        x_copy(2 + i, psend.at[1, high, at], pre.at[1, :, at], left)
        for i, at in enumerate(halves)
    ]
    x_right = x_copy(4, psend.at[2, high], full.at[0, high], right)
    x_left = x_copy(5, psend.at[0, low], full.at[1, low], left)
    x_join_right = [
        x_copy(6 + i, psend.at[2, low, at], full.at[0, low, at], right)
        for i, at in enumerate(halves)
    ]
    x_join_left = [
        x_copy(8 + i, psend.at[0, high, at], full.at[1, high, at], left)
        for i, at in enumerate(halves)
    ]

    def join(index, part, slot, at):
        psend[index, part, at] = (
            widen(psend[index, part, at]) + widen(pre[slot, :, at])
        ).astype(jnp.bfloat16)

    for copy in load_w:
        copy.wait()
    load_tab.wait()
    for copy in load_kv:
        copy.start()
    load_wo.start()
    stage((0,), 0, 1)
    ag_copies[0].wait_recv()
    ag_copies[4].start()
    ag_copies[1].wait_recv()
    ag_copies[5].start()
    relay(0)
    for copy in load_kv:
        copy.wait()
    prepare()
    pass_on(0)
    ag_copies[2].wait_recv()
    ag_copies[3].wait_recv()
    stage((1, 3), 1, 2)
    relay(1)
    relay(3)
    ag_copies[4].wait_recv()
    ag_copies[5].wait_recv()
    stage((2,), 3, 1)
    for s in range(4):
        attend_new(s)
    relay(2)
    arrive(0)
    attend((0,), 0, 4, 2)
    pass_on(1)
    pass_on(3)
    arrive(1)
    arrive(3)
    attend((1, 3), 0, 8, 1)
    exchange(1)
    exchange(3)
    pass_on(2)
    arrive(2)
    attend((2,), 0, 4, 2)
    pair_up(1)
    pair_up(3)
    attend((2,), 4, 8, 2)
    exchange(2)
    load_wo.wait()
    to_send(1)
    x_left.start()
    to_send(3)
    x_right.start()
    pair_up(2)
    attend((0,), 4, 8, 2)
    exchange(0)
    to_send(2)
    for i in range(2):
        x_far_low[i].start()
        x_far_high[i].start()
    pair_up(0)
    for i, at in enumerate(halves):
        x_far_low[i].wait_recv()
        join(2, low, 0, at)
        x_join_right[i].start()
        x_far_high[i].wait_recv()
        join(0, high, 1, at)
        x_join_left[i].start()

    def keep(at, value):
        total[:, at] = widen(tok[:, at]) + widen(value.astype(jnp.bfloat16))

    outward(0, keep)
    x_right.wait_recv()
    x_left.wait_recv()
    for i in range(2):
        x_join_right[i].wait_recv()
        x_join_left[i].wait_recv()
    out_ref[...] = (total[...] + widen(full[0]) + widen(full[1])).astype(jnp.bfloat16)

    for copy in ag_copies + x_far_low + x_far_high + x_join_left + x_join_right:
        copy.wait_send()
    x_left.wait_send()
    x_right.wait_send()
    for s in range(4):
        y_copy(s).wait_send()
        p_copy(s, qprev.at[s]).wait_send()
        d_copy(s).wait_send()
        ds_copy(s).wait_send()
        for dz in dzs:
            z_copy(dz, s, qprev.at[s]).wait_send()
            f_copy(dz, s).wait_send()
            m_copy(dz, s).wait_send()
            ms_copy(dz, s).wait_send()
            r_copy(dz, s).wait_send()
            rs_copy(dz, s).wait_send()


def turn_tables(head_dim, count):
    freqs = rope_base ** (-np.arange(head_dim // 2) * 2.0 / head_dim)
    steps = np.concatenate([128.0 * np.arange(coarse_rows), np.arange(count)])
    angles = steps[:, None] * freqs[None, :]
    cosine, sine = np.cos(angles), np.sin(angles)
    return np.stack(
        [np.concatenate([cosine, cosine], axis=1), np.concatenate([-sine, sine], axis=1)]
    ).astype(np.float32)


def on_device(
    tokens,
    norm_gain,
    w_query,
    w_key,
    w_value,
    query_gain,
    key_gain,
    w_out,
    cache_keys,
    cache_values,
    cache_plan,
):
    hd = query_gain.shape[0]
    rows, depth = tokens.shape
    qw = w_query.shape[1]
    spread = cache_plan.shape[1]
    n_tp = lax.axis_size("tp")
    count = rows * n_tp
    tall = qw // hd * rows
    gains = jnp.concatenate([norm_gain, query_gain, key_gain]).astype(jnp.float32)[None, :]
    tables = jnp.asarray(turn_tables(hd, max(count, 128)))
    vm = pl.BlockSpec(memory_space=pltpu.VMEM)
    hbm = pl.BlockSpec(memory_space=pltpu.HBM)
    bf16, f32 = jnp.bfloat16, jnp.float32
    dma = pltpu.SemaphoreType.DMA
    return pl.pallas_call(
        functools.partial(kernel, hd ** (-0.5) * log2e),
        out_shape=jax.ShapeDtypeStruct((rows, depth), bf16),
        in_specs=[pl.BlockSpec(memory_space=pltpu.SMEM), vm] + [hbm] * 8,
        out_specs=vm,
        scratch_shapes=[
            pltpu.VMEM(tables.shape, f32),
            pltpu.VMEM((rows, depth), bf16),
            pltpu.VMEM((n_tp, rows, depth), bf16),
            pltpu.VMEM((depth, qw + 2 * hd), bf16),
            pltpu.VMEM(w_out.shape, bf16),
            pltpu.VMEM((2 * rows, qw + 2 * hd), f32),
            pltpu.VMEM(cache_keys.shape, bf16),
            pltpu.VMEM((cache_keys.shape[0], 2 * hd), bf16),
            pltpu.VMEM((count, hd), bf16),
            pltpu.VMEM((count, 2 * hd), bf16),
            pltpu.VMEM((spread, n_tp, tall, hd), bf16),
            pltpu.VMEM((n_tp, tall, hd), bf16),
            pltpu.VMEM((spread, n_tp, tall, hd), bf16),
            pltpu.VMEM((n_tp, tall, hd), bf16),
            pltpu.VMEM((spread + 1, n_tp, 8, hd), f32),
            pltpu.VMEM((3, n_tp, tall, hd), bf16),
            pltpu.VMEM((3, n_tp, 8, hd), f32),
            pltpu.VMEM((n_tp, tall, hd), bf16),
            pltpu.VMEM((n_tp, 8, hd), f32),
            pltpu.VMEM((3, n_tp, tall, hd), bf16),
            pltpu.VMEM((3, n_tp, 8, hd), f32),
            pltpu.VMEM((3, n_tp, tall, hd), bf16),
            pltpu.VMEM((3, n_tp, 8, hd), f32),
            pltpu.VMEM((3, rows, depth), bf16),
            pltpu.VMEM((2, rows // 2, depth), bf16),
            pltpu.VMEM((2, rows, depth), bf16),
            pltpu.VMEM((rows, depth), f32),
            dma((8,)),
            dma((6,)),
            dma((6,)),
            dma((4,)),
            dma((4,)),
            dma((3, 4)),
            dma((3, 4)),
            dma((4,)),
            dma((4,)),
            dma((3, 4)),
            dma((3, 4)),
            dma((3, 4)),
            dma((3, 4)),
            dma((3, 4)),
            dma((3, 4)),
            dma((4,)),
            dma((4,)),
            dma((4,)),
            dma((4,)),
            dma((3, 4)),
            dma((3, 4)),
            dma((3, 4)),
            dma((3, 4)),
            dma((10,)),
            dma((10,)),
        ],
        compiler_params=pltpu.CompilerParams(
            collective_id=0, has_side_effects=True, vmem_limit_bytes=66 * 1000 * 1000
        ),
    )(
        cache_plan,
        gains,
        tables,
        tokens,
        w_query,
        w_key,
        w_value,
        w_out,
        cache_keys,
        cache_values,
    )


def solution(mesh):
    placed = (
        P(("req", "tp"), None),
        P(),
        P(None, "tp"),
        P(None, "tp"),
        P(None, "tp"),
        P(),
        P(),
        P("tp", None),
        P("req", "tp"),
        P("req", "tp"),
        P(),
    )
    return jax.shard_map(
        on_device, mesh=mesh, in_specs=placed, out_specs=P(("req", "tp"), None), check_vma=False
    )
```

```python
import functools
import jax
import jax.numpy as jnp
import numpy as np
from jax import lax
from jax.experimental import pallas as pl
from jax.experimental.pallas import tpu as pltpu
from jax.sharding import PartitionSpec as P

norm_eps = 1e-06
rope_base = 1000000.0
log2e = 1.4426950408889634
NEG = -1e30
MESH = pl.DeviceIdType.MESH
coarse_rows = 136


def widen(value):
    return value.astype(jnp.float32)


def remote(src, dst, send, recv, req, tp):
    return pltpu.make_async_remote_copy(
        src_ref=src,
        dst_ref=dst,
        send_sem=send,
        recv_sem=recv,
        device_id=(req, tp),
        device_id_type=MESH,
    )


def kernel(
    score_scale,
    plan_ref,
    ng_hbm,
    qg_hbm,
    kg_hbm,
    tab_hbm,
    tok_hbm,
    wq_hbm,
    wk_hbm,
    wv_hbm,
    wo_hbm,
    k_hbm,
    v_hbm,
    out_ref,
    tab,
    gains,
    head_gains,
    tok,
    xs,
    w,
    wo,
    acc,
    kx,
    vx,
    nk,
    nv,
    qs,
    qprev,
    obuf,
    onew,
    stat,
    mbuf,
    mst,
    dbuf,
    dst,
    sbuf,
    sst,
    rbuf,
    rst,
    psend,
    pre,
    full,
    total,
    load_sem,
    ag_send,
    ag_recv,
    y_send,
    y_recv,
    z_send,
    z_recv,
    p_send,
    p_recv,
    f_send,
    f_recv,
    m_send,
    m_recv,
    ms_send,
    ms_recv,
    d_send,
    d_recv,
    ds_send,
    ds_recv,
    r_send,
    r_recv,
    rs_send,
    rs_recv,
    x_send,
    x_recv,
):
    req, tp = lax.axis_index("req"), lax.axis_index("tp")
    n_req, n_tp = lax.axis_size("req"), lax.axis_size("tp")
    core = lax.rem(req, 2)
    z = lax.rem(req // 2, 4)
    plane = req - 2 * z - core
    rows, depth = tok.shape
    half = rows // 2
    spread = plan_ref.shape[0]
    cap = kx.shape[0] // spread
    hd = kx.shape[1]
    qw = wo.shape[0]
    heads = qw // hd
    tall = heads * rows
    right, left = lax.rem(tp + 1, n_tp), lax.rem(tp + n_tp - 1, n_tp)
    mate = req + 1 - 2 * core
    lone = 7 - 6 * core
    dzs = (1, 2, 3)

    def ahead(steps):
        return lax.rem(req + n_req + steps, n_req)

    def z_peer(dz):
        return plane + 2 * lax.rem(z + dz, 4) + core

    def load(index, src, target):
        return pltpu.make_async_copy(src, target, load_sem.at[index])

    low, high = slice(0, half), slice(half, rows)
    load_tok = [load(0, tok_hbm.at[low], tok.at[low]), load(8, tok_hbm.at[high], tok.at[high])]
    lanes_of = depth // hd
    load_gains = [
        load(9, ng_hbm, gains),
        load(10, qg_hbm, head_gains.at[0]),
        load(11, kg_hbm, head_gains.at[1]),
    ]
    load_w = [
        load(1, wq_hbm, w.at[:, :qw]),
        load(2, wk_hbm, w.at[:, qw : qw + hd]),
        load(3, wv_hbm, w.at[:, qw + hd :]),
    ]
    load_tab = load(4, tab_hbm, tab)
    load_kv = [load(5, k_hbm, kx), load(6, v_hbm, vx.at[:, :hd])]
    load_wo = load(7, wo_hbm, wo)
    for copy in load_tok + load_gains + load_w:
        copy.start()
    load_tab.start()

    barrier = pltpu.get_barrier_semaphore()
    partners = [(req, right), (req, left), (mate, tp), (ahead(14 * core - 7), tp)]
    partners += [(ahead(steps), tp) for steps in (8, -8, 2, 4, 6, -2, -4, -6)]
    partners += [(z_peer(dz), tp) for dz in dzs]
    for where in partners:
        pl.semaphore_signal(barrier, inc=1, device_id=where, device_id_type=MESH)

    for copy in load_gains:
        copy.wait()
    gain = widen(gains[...])
    q_gain = widen(head_gains[0]) * score_scale
    k_gain = widen(head_gains[1])

    def normalize(part, load_part):
        load_part.wait()
        value = widen(tok[part])
        scale = lax.rsqrt(jnp.mean(value * value, axis=-1, keepdims=True) + norm_eps)
        for n in range(lanes_of):
            at = slice(n * hd, (n + 1) * hd)
            xs[0, part, at] = (value[:, at] * scale * gain[n : n + 1]).astype(jnp.bfloat16)

    normalize(low, load_tok[0])
    pl.semaphore_wait(barrier, len(partners))

    def ag(index, at_from, at_to, part, target):
        return remote(
            xs.at[at_from, part],
            xs.at[at_to, part],
            ag_send.at[index],
            ag_recv.at[index],
            req,
            target,
        )

    ag_copies = [
        ag(0, 0, 1, low, right),
        ag(1, 0, 2, high, left),
        ag(2, 0, 1, high, right),
        ag(3, 0, 2, low, left),
        ag(4, 1, 3, low, right),
        ag(5, 2, 3, high, left),
    ]
    ag_copies[0].start()
    normalize(high, load_tok[1])
    for copy in ag_copies[1:4]:
        copy.start()

    def first_row(s):
        return pl.multiple_of(lax.rem(tp + n_tp - s, n_tp) * rows, rows)

    def y_copy(s):
        return remote(qs.at[0, s], qprev.at[s], y_send.at[s], y_recv.at[s], ahead(8), tp)

    def z_copy(dz, s, src):
        return remote(
            src, qs.at[2 * dz, s], z_send.at[dz - 1, s], z_recv.at[dz - 1, s], z_peer(dz), tp
        )

    def p_copy(s, src):
        return remote(src, qs.at[1 + 6 * core, s], p_send.at[s], p_recv.at[s], mate, tp)

    def f_copy(dz, s):
        return remote(
            qs.at[2 * dz, s],
            qs.at[2 * dz + 1 - 2 * core, s],
            f_send.at[dz - 1, s],
            f_recv.at[dz - 1, s],
            mate,
            tp,
        )

    length = plan_ref[0, req]
    for k in range(1, spread):
        length += plan_ref[k, req]
    coarse = length // 128
    fine = coarse_rows + length - coarse * 128

    def stage(blocks, at, n):
        width = depth // 5
        acc[: n * rows] = jnp.zeros((n * rows, acc.shape[1]), jnp.float32)

        def block(b, carry):
            cols = pl.ds(pl.multiple_of(b * width, width), width)
            left_side = xs[at : at + n, :, cols].reshape(n * rows, width)
            acc[: n * rows] += jnp.dot(
                left_side, w[cols, :], preferred_element_type=jnp.float32
            )
            return carry

        lax.fori_loop(0, 5, block, 0)
        c_a, s_a = tab[0, pl.ds(coarse, 1), :], tab[1, pl.ds(coarse, 1), :]
        c_b, s_b = tab[0, pl.ds(fine, 1), :], tab[1, pl.ds(fine, 1), :]
        c_l, s_l = c_a * c_b - s_a * s_b, s_a * c_b + c_a * s_b
        for i, s in enumerate(blocks):
            here = pl.ds(first_row(s), rows)
            there = pl.ds(pl.multiple_of(coarse_rows + first_row(s), 8), rows)
            c_t, s_t = tab[0, there, :], tab[1, there, :]
            cosine, sine = c_t * c_l - s_t * s_l, s_t * c_l + c_t * s_l

            def turned(col, gain):
                head = acc[i * rows : (i + 1) * rows, col : col + hd]
                mean = jnp.mean(head * head, axis=-1, keepdims=True)
                head = head * lax.rsqrt(mean + norm_eps) * gain
                return (head * cosine + pltpu.roll(head, hd // 2, 1) * sine).astype(
                    jnp.bfloat16
                )

            for h in range(heads):
                qs[0, s, h * rows : (h + 1) * rows] = turned(h * hd, q_gain)
            nk[here, :] = turned(qw, k_gain)
            nv[here, :hd] = acc[i * rows : (i + 1) * rows, qw + hd :].astype(jnp.bfloat16)
            y_copy(s).start()
            for dz in dzs:

                @pl.when(z + dz < 4)
                def _():
                    z_copy(dz, s, qs.at[0, s]).start()

            @pl.when(core == 0)
            def _():
                p_copy(s, qs.at[0, s]).start()

    def relay(s):
        y_copy(s).wait_recv()
        for dz in dzs:

            @pl.when(z + dz >= 4)
            def _():
                z_copy(dz, s, qprev.at[s]).start()

        @pl.when(core == 1)
        def _():
            p_copy(s, qprev.at[s]).start()

    def pass_on(s):
        for dz in dzs:
            z_copy(dz, s, qprev.at[s]).wait_recv()
            f_copy(dz, s).start()

    def arrive(s):
        p_copy(s, qprev.at[s]).wait_recv()
        for dz in dzs:
            f_copy(dz, s).wait_recv()

    def softmax(scores, values):
        top = jnp.max(scores, axis=1, keepdims=True)
        weights = jnp.exp2(scores - top).astype(jnp.bfloat16)
        both = jnp.dot(weights, values, preferred_element_type=jnp.float32)
        return both[:, :hd], both[:, hd:], top

    def dot_t(a, b):
        return lax.dot_general(a, b, (((1,), (1,)), ((), ())), preferred_element_type=jnp.float32)

    lanes = lax.broadcasted_iota(jnp.int32, (rows, hd), 1)

    def settle(parts):
        summed = jnp.concatenate([one[0] for one in parts], axis=0)
        mass = jnp.concatenate([one[1] for one in parts], axis=0)
        top = jnp.concatenate([one[2] for one in parts], axis=0)
        some = mass > 0
        value = jnp.where(some, summed / mass, 0.0).astype(jnp.bfloat16)
        level = jnp.where(some, top + jnp.log2(mass), NEG)
        table = jnp.full((rows, hd), NEG, jnp.float32)
        for h in range(heads):
            table = jnp.where(lanes == h, level[h * rows : (h + 1) * rows], table)
        table = jnp.concatenate([table, jnp.zeros_like(table)], axis=0)
        return value, jnp.transpose(table)[:8]

    def attend(blocks, first, last, unroll):
        sub = tall // 2

        def piece(k, carry):
            keys = kx[pl.ds(pl.multiple_of(k * cap, cap), cap), :]
            values = vx[pl.ds(pl.multiple_of(k * cap, cap), cap), :]
            scores = [
                dot_t(qs[k, s, n * sub : (n + 1) * sub], keys) for s in blocks for n in range(2)
            ]
            done = [softmax(one, values) for one in scores]
            for i, s in enumerate(blocks):
                obuf[k, s], stat[k, s] = settle(done[2 * i : 2 * i + 2])
            return carry

        lax.fori_loop(first, last, piece, 0, unroll=unroll)

    def attend_new(s):
        scores = dot_t(qs[0, s], nk[...])
        row = lax.broadcasted_iota(jnp.int32, scores.shape, 0)
        row = first_row(s) + jnp.bitwise_and(row, rows - 1)
        col = lax.broadcasted_iota(jnp.int32, scores.shape, 1)
        scores = jnp.where(row >= col, scores, NEG)
        onew[s], stat[spread, s] = settle([softmax(scores, nv[...])])

    def prepare():
        def piece(k, carry):
            at = pl.ds(pl.multiple_of(k * cap, cap), cap)
            count = plan_ref[k, lax.rem(req + n_req - k, n_req)]
            row = lax.broadcasted_iota(jnp.int32, (cap, hd), 0)
            ok = row < count
            keys = kx[at, :]
            kx[at, :] = jnp.where(ok, keys, jnp.broadcast_to(keys[0:1], keys.shape))
            vx[at, :hd] = jnp.where(ok, vx[at, :hd], jnp.zeros((cap, hd), jnp.bfloat16))
            vx[at, hd:] = jnp.where(ok, 1.0, 0.0).astype(jnp.bfloat16)
            return carry

        lax.fori_loop(0, spread, piece, 0)
        nv[:, hd:] = jnp.ones((nv.shape[0], hd), jnp.bfloat16)

    def m_copy(dz, s):
        return remote(
            obuf.at[2 * dz - 1 + 2 * core, s],
            mbuf.at[dz - 1, s],
            m_send.at[dz - 1, s],
            m_recv.at[dz - 1, s],
            mate,
            tp,
        )

    def ms_copy(dz, s):
        return remote(
            stat.at[2 * dz - 1 + 2 * core, s],
            mst.at[dz - 1, s],
            ms_send.at[dz - 1, s],
            ms_recv.at[dz - 1, s],
            mate,
            tp,
        )

    def d_copy(s):
        return remote(obuf.at[lone, s], dbuf.at[s], d_send.at[s], d_recv.at[s], ahead(-lone), tp)

    def ds_copy(s):
        return remote(stat.at[lone, s], dst.at[s], ds_send.at[s], ds_recv.at[s], ahead(-lone), tp)

    def r_copy(dz, s):
        return remote(
            sbuf.at[dz - 1, s],
            rbuf.at[dz - 1, s],
            r_send.at[dz - 1, s],
            r_recv.at[dz - 1, s],
            ahead(-2 * dz),
            tp,
        )

    def rs_copy(dz, s):
        return remote(
            sst.at[dz - 1, s],
            rst.at[dz - 1, s],
            rs_send.at[dz - 1, s],
            rs_recv.at[dz - 1, s],
            ahead(-2 * dz),
            tp,
        )

    def exchange(s):
        for dz in dzs:
            ms_copy(dz, s).start()
            m_copy(dz, s).start()
        ds_copy(s).start()
        d_copy(s).start()

    def columns(pieces):
        pad = jnp.zeros((128 - 8 * len(pieces), hd), jnp.float32)
        return jnp.transpose(jnp.concatenate(pieces + [pad], axis=0))[:rows]

    def pair_up(s):
        for dz in dzs:
            ms_copy(dz, s).wait_recv()
        shares = []
        for dz in dzs:
            mine, other = stat[2 * dz, s], mst[dz - 1, s]
            top = jnp.maximum(mine, other)
            mine, other = jnp.exp2(mine - top), jnp.exp2(other - top)
            mass = mine + other
            sst[dz - 1, s] = top + jnp.log2(mass)
            shares += [mine / mass, other / mass]
        table = columns(shares)
        for dz in dzs:
            m_copy(dz, s).wait_recv()
            for h in range(heads):
                at = slice(h * rows, (h + 1) * rows)
                i, j = 16 * (dz - 1) + h, 16 * (dz - 1) + 8 + h
                both = widen(obuf[2 * dz, s, at]) * table[:, i : i + 1]
                both += widen(mbuf[dz - 1, s, at]) * table[:, j : j + 1]
                sbuf[dz - 1, s, at] = both.astype(jnp.bfloat16)
            rs_copy(dz, s).start()
            r_copy(dz, s).start()

    def merged(s):
        ds_copy(s).wait_recv()
        d_copy(s).wait_recv()
        for dz in dzs:
            rs_copy(dz, s).wait_recv()
            r_copy(dz, s).wait_recv()
        tops = [stat[spread, s], stat[0, s], dst[s]] + [rst[dz - 1, s] for dz in dzs]
        top = functools.reduce(jnp.maximum, tops)
        masses = [jnp.exp2(one - top) for one in tops]
        mass = functools.reduce(jnp.add, masses)
        table = columns([one / mass for one in masses])
        heads_out = []
        for h in range(heads):
            at = slice(h * rows, (h + 1) * rows)
            sources = [onew[s, at], obuf[0, s, at], dbuf[s, at]]
            sources += [rbuf[dz - 1, s, at] for dz in dzs]
            value = jnp.zeros((rows, hd), jnp.float32)
            for n, source in enumerate(sources):
                i = 8 * n + h
                value += widen(source) * table[:, i : i + 1]
            heads_out.append(value.astype(jnp.bfloat16))
        return jnp.concatenate(heads_out, axis=1)

    def project(attended, store):
        width = depth // 5

        def tile(b, carry):
            at = pl.ds(pl.multiple_of(b * width, width), width)
            store(at, jnp.dot(attended, wo[:, at], preferred_element_type=jnp.float32))
            return carry

        lax.fori_loop(0, 5, tile, 0)

    def x_copy(index, src, target_ref, target):
        return remote(src, target_ref, x_send.at[index], x_recv.at[index], req, target)

    width = depth // 5
    tiles = [slice(n * width, (n + 1) * width) for n in range(5)]
    x_far_low = [
        x_copy(n, psend.at[1, low, at], pre.at[0, :, at], right) for n, at in enumerate(tiles)
    ]
    x_far_high = [
        x_copy(5 + n, psend.at[1, high, at], pre.at[1, :, at], left)
        for n, at in enumerate(tiles)
    ]
    x_join_right = [
        x_copy(10 + n, psend.at[2, low, at], full.at[0, low, at], right)
        for n, at in enumerate(tiles)
    ]
    x_join_left = [
        x_copy(15 + n, psend.at[0, high, at], full.at[1, high, at], left)
        for n, at in enumerate(tiles)
    ]
    x_right = x_copy(20, psend.at[2, high], full.at[0, high], right)
    x_left = x_copy(21, psend.at[0, low], full.at[1, low], left)

    def join(index, part, slot, at):
        psend[index, part, at] = (
            widen(psend[index, part, at]) + widen(pre[slot, :, at])
        ).astype(jnp.bfloat16)

    for copy in load_w:
        copy.wait()
    load_tab.wait()
    for copy in load_kv:
        copy.start()
    load_wo.start()
    stage((0,), 0, 1)
    ag_copies[0].wait_recv()
    ag_copies[4].start()
    ag_copies[1].wait_recv()
    ag_copies[5].start()
    relay(0)
    for copy in load_kv:
        copy.wait()
    prepare()
    pass_on(0)
    ag_copies[2].wait_recv()
    ag_copies[3].wait_recv()
    stage((1, 3), 1, 2)
    arrive(0)
    attend((0,), 0, 4, 2)
    relay(1)
    relay(3)
    ag_copies[4].wait_recv()
    ag_copies[5].wait_recv()
    stage((2,), 3, 1)
    attend((0,), 4, 8, 2)
    exchange(0)
    pass_on(1)
    pass_on(3)
    relay(2)
    arrive(1)
    arrive(3)
    attend((1, 3), 0, 4, 1)
    pass_on(2)
    pair_up(0)
    attend((1, 3), 4, 8, 1)
    exchange(1)
    exchange(3)
    arrive(2)
    attend((2,), 0, 2, 2)
    pair_up(1)
    pair_up(3)
    attend((2,), 2, 8, 2)
    exchange(2)
    load_wo.wait()
    attend_new(1)
    attend_new(3)
    attend_new(2)
    pair_up(2)
    attended_1 = merged(1)
    attended_3 = merged(3)

    def store_pair(at, value):
        psend[0, :, at] = value[:rows].astype(jnp.bfloat16)
        psend[2, :, at] = value[rows:].astype(jnp.bfloat16)

    project(jnp.concatenate([attended_1, attended_3], axis=0), store_pair)
    x_left.start()
    x_right.start()
    attended_2 = merged(2)
    for n, at in enumerate(tiles):
        value = jnp.dot(attended_2, wo[:, at], preferred_element_type=jnp.float32)
        psend[1, :, at] = value.astype(jnp.bfloat16)
        if n:
            x_far_low[n - 1].start()
            x_far_high[n - 1].start()
    x_far_low[-1].start()
    x_far_high[-1].start()

    def keep(at, value):
        total[:, at] = widen(tok[:, at]) + widen(value.astype(jnp.bfloat16))

    attend_new(0)
    project(merged(0), keep)
    for n, at in enumerate(tiles):
        x_far_low[n].wait_recv()
        join(2, low, 0, at)
        x_far_high[n].wait_recv()
        join(0, high, 1, at)
        x_join_right[n].start()
        x_join_left[n].start()
    x_right.wait_recv()
    x_left.wait_recv()
    for n, at in enumerate(tiles):
        x_join_right[n].wait_recv()
        x_join_left[n].wait_recv()
        out_ref[:, at] = (
            total[:, at] + widen(full[0, :, at]) + widen(full[1, :, at])
        ).astype(jnp.bfloat16)

    for copy in ag_copies + x_far_low + x_far_high + x_join_left + x_join_right:
        copy.wait_send()
    x_left.wait_send()
    x_right.wait_send()
    for s in range(4):
        y_copy(s).wait_send()
        p_copy(s, qprev.at[s]).wait_send()
        d_copy(s).wait_send()
        ds_copy(s).wait_send()
        for dz in dzs:
            z_copy(dz, s, qprev.at[s]).wait_send()
            f_copy(dz, s).wait_send()
            m_copy(dz, s).wait_send()
            ms_copy(dz, s).wait_send()
            r_copy(dz, s).wait_send()
            rs_copy(dz, s).wait_send()


def turn_tables(head_dim, count):
    freqs = rope_base ** (-np.arange(head_dim // 2) * 2.0 / head_dim)
    steps = np.concatenate([128.0 * np.arange(coarse_rows), np.arange(count)])
    angles = steps[:, None] * freqs[None, :]
    cosine, sine = np.cos(angles), np.sin(angles)
    return np.stack(
        [np.concatenate([cosine, cosine], axis=1), np.concatenate([-sine, sine], axis=1)]
    ).astype(np.float32)


def on_device(
    tokens,
    norm_gain,
    w_query,
    w_key,
    w_value,
    query_gain,
    key_gain,
    w_out,
    cache_keys,
    cache_values,
    cache_plan,
):
    hd = query_gain.shape[0]
    rows, depth = tokens.shape
    qw = w_query.shape[1]
    spread = cache_plan.shape[1]
    n_tp = lax.axis_size("tp")
    count = rows * n_tp
    tall = qw // hd * rows
    tables = jnp.asarray(turn_tables(hd, max(count, 128)))
    vm = pl.BlockSpec(memory_space=pltpu.VMEM)
    hbm = pl.BlockSpec(memory_space=pltpu.HBM)
    bf16, f32 = jnp.bfloat16, jnp.float32
    dma = pltpu.SemaphoreType.DMA
    return pl.pallas_call(
        functools.partial(kernel, hd ** (-0.5) * log2e),
        out_shape=jax.ShapeDtypeStruct((rows, depth), bf16),
        in_specs=[pl.BlockSpec(memory_space=pltpu.SMEM)] + [hbm] * 11,
        out_specs=vm,
        scratch_shapes=[
            pltpu.VMEM(tables.shape, f32),
            pltpu.VMEM((depth // hd, hd), bf16),
            pltpu.VMEM((2, 1, hd), bf16),
            pltpu.VMEM((rows, depth), bf16),
            pltpu.VMEM((n_tp, rows, depth), bf16),
            pltpu.VMEM((depth, qw + 2 * hd), bf16),
            pltpu.VMEM(w_out.shape, bf16),
            pltpu.VMEM((2 * rows, qw + 2 * hd), f32),
            pltpu.VMEM(cache_keys.shape, bf16),
            pltpu.VMEM((cache_keys.shape[0], 2 * hd), bf16),
            pltpu.VMEM((count, hd), bf16),
            pltpu.VMEM((count, 2 * hd), bf16),
            pltpu.VMEM((spread, n_tp, tall, hd), bf16),
            pltpu.VMEM((n_tp, tall, hd), bf16),
            pltpu.VMEM((spread, n_tp, tall, hd), bf16),
            pltpu.VMEM((n_tp, tall, hd), bf16),
            pltpu.VMEM((spread + 1, n_tp, 8, hd), f32),
            pltpu.VMEM((3, n_tp, tall, hd), bf16),
            pltpu.VMEM((3, n_tp, 8, hd), f32),
            pltpu.VMEM((n_tp, tall, hd), bf16),
            pltpu.VMEM((n_tp, 8, hd), f32),
            pltpu.VMEM((3, n_tp, tall, hd), bf16),
            pltpu.VMEM((3, n_tp, 8, hd), f32),
            pltpu.VMEM((3, n_tp, tall, hd), bf16),
            pltpu.VMEM((3, n_tp, 8, hd), f32),
            pltpu.VMEM((3, rows, depth), bf16),
            pltpu.VMEM((2, rows // 2, depth), bf16),
            pltpu.VMEM((2, rows, depth), bf16),
            pltpu.VMEM((rows, depth), f32),
            dma((12,)),
            dma((6,)),
            dma((6,)),
            dma((4,)),
            dma((4,)),
            dma((3, 4)),
            dma((3, 4)),
            dma((4,)),
            dma((4,)),
            dma((3, 4)),
            dma((3, 4)),
            dma((3, 4)),
            dma((3, 4)),
            dma((3, 4)),
            dma((3, 4)),
            dma((4,)),
            dma((4,)),
            dma((4,)),
            dma((4,)),
            dma((3, 4)),
            dma((3, 4)),
            dma((3, 4)),
            dma((3, 4)),
            dma((22,)),
            dma((22,)),
        ],
        compiler_params=pltpu.CompilerParams(
            collective_id=0, has_side_effects=True, vmem_limit_bytes=64 * 1000 * 1000
        ),
    )(
        cache_plan.T,
        norm_gain.reshape(depth // hd, hd),
        query_gain.reshape(1, hd),
        key_gain.reshape(1, hd),
        tables,
        tokens,
        w_query,
        w_key,
        w_value,
        w_out,
        cache_keys,
        cache_values,
    )


def solution(mesh):
    placed = (
        P(("req", "tp"), None),
        P(),
        P(None, "tp"),
        P(None, "tp"),
        P(None, "tp"),
        P(),
        P(),
        P("tp", None),
        P("req", "tp"),
        P("req", "tp"),
        P(),
    )
    return jax.shard_map(
        on_device, mesh=mesh, in_specs=placed, out_specs=P(("req", "tp"), None), check_vma=False
    )
```

```python
import functools
import jax
import jax.numpy as jnp
import numpy as np
from jax import lax
from jax.experimental import pallas as pl
from jax.experimental.pallas import tpu as pltpu
from jax.sharding import PartitionSpec as P

norm_eps = 1e-06
rope_base = 1000000.0
log2e = 1.4426950408889634
NEG = -1e30
MESH = pl.DeviceIdType.MESH
coarse_rows = 136


def widen(value):
    return value.astype(jnp.float32)


def remote(src, dst, send, recv, req, tp):
    return pltpu.make_async_remote_copy(
        src_ref=src,
        dst_ref=dst,
        send_sem=send,
        recv_sem=recv,
        device_id=(req, tp),
        device_id_type=MESH,
    )


def kernel(
    score_scale,
    plan_ref,
    ng_hbm,
    qg_hbm,
    kg_hbm,
    tab_hbm,
    tok_hbm,
    wq_hbm,
    wk_hbm,
    wv_hbm,
    wo_hbm,
    k_hbm,
    v_hbm,
    out_ref,
    tab,
    gains,
    head_gains,
    tok,
    xs,
    w,
    wo,
    acc,
    kx,
    vx,
    nk,
    nv,
    qs,
    qprev,
    obuf,
    onew,
    stat,
    mbuf,
    mst,
    dbuf,
    dst,
    sbuf,
    sst,
    rbuf,
    rst,
    psend,
    pre,
    full,
    total,
    load_sem,
    ag_send,
    ag_recv,
    y_send,
    y_recv,
    z_send,
    z_recv,
    p_send,
    p_recv,
    f_send,
    f_recv,
    m_send,
    m_recv,
    ms_send,
    ms_recv,
    d_send,
    d_recv,
    ds_send,
    ds_recv,
    r_send,
    r_recv,
    rs_send,
    rs_recv,
    x_send,
    x_recv,
):
    req, tp = lax.axis_index("req"), lax.axis_index("tp")
    n_req, n_tp = lax.axis_size("req"), lax.axis_size("tp")
    core = lax.rem(req, 2)
    z = lax.rem(req // 2, 4)
    plane = req - 2 * z - core
    rows, depth = tok.shape
    half = rows // 2
    spread = plan_ref.shape[0]
    cap = kx.shape[0] // spread
    hd = kx.shape[1]
    qw = wo.shape[0]
    heads = qw // hd
    tall = heads * rows
    right, left = lax.rem(tp + 1, n_tp), lax.rem(tp + n_tp - 1, n_tp)
    mate = req + 1 - 2 * core
    lone = 7 - 6 * core
    dzs = (1, 2, 3)

    def ahead(steps):
        return lax.rem(req + n_req + steps, n_req)

    def z_peer(dz):
        return plane + 2 * lax.rem(z + dz, 4) + core

    def load(index, src, target):
        return pltpu.make_async_copy(src, target, load_sem.at[index])

    low, high = slice(0, half), slice(half, rows)
    load_tok = [load(0, tok_hbm.at[low], tok.at[low]), load(8, tok_hbm.at[high], tok.at[high])]
    lanes_of = depth // hd
    load_gains = [
        load(9, ng_hbm, gains),
        load(10, qg_hbm, head_gains.at[0]),
        load(11, kg_hbm, head_gains.at[1]),
    ]
    load_w = [
        load(1, wq_hbm, w.at[:, :qw]),
        load(2, wk_hbm, w.at[:, qw : qw + hd]),
        load(3, wv_hbm, w.at[:, qw + hd :]),
    ]
    load_tab = load(4, tab_hbm, tab)
    load_kv = [load(5, k_hbm, kx), load(6, v_hbm, vx.at[:, :hd])]
    load_wo = load(7, wo_hbm, wo)
    for copy in load_tok + load_gains + load_w:
        copy.start()
    load_tab.start()

    barrier = pltpu.get_barrier_semaphore()
    partners = [(req, right), (req, left), (mate, tp), (ahead(14 * core - 7), tp)]
    partners += [(ahead(steps), tp) for steps in (8, -8, 2, 4, 6, -2, -4, -6)]
    partners += [(z_peer(dz), tp) for dz in dzs]
    for where in partners:
        pl.semaphore_signal(barrier, inc=1, device_id=where, device_id_type=MESH)

    for copy in load_gains:
        copy.wait()
    gain = widen(gains[...])
    q_gain = widen(head_gains[0]) * score_scale
    k_gain = widen(head_gains[1])

    def normalize(part, load_part):
        load_part.wait()
        value = widen(tok[part])
        scale = lax.rsqrt(jnp.mean(value * value, axis=-1, keepdims=True) + norm_eps)
        for n in range(lanes_of):
            at = slice(n * hd, (n + 1) * hd)
            xs[0, part, at] = (value[:, at] * scale * gain[n : n + 1]).astype(jnp.bfloat16)

    normalize(low, load_tok[0])
    pl.semaphore_wait(barrier, len(partners))

    def ag(index, at_from, at_to, part, target):
        return remote(
            xs.at[at_from, part],
            xs.at[at_to, part],
            ag_send.at[index],
            ag_recv.at[index],
            req,
            target,
        )

    ag_copies = [
        ag(0, 0, 1, low, right),
        ag(1, 0, 2, high, left),
        ag(2, 0, 1, high, right),
        ag(3, 0, 2, low, left),
        ag(4, 1, 3, low, right),
        ag(5, 2, 3, high, left),
    ]
    ag_copies[0].start()
    normalize(high, load_tok[1])
    for copy in ag_copies[1:4]:
        copy.start()

    def first_row(s):
        return pl.multiple_of(lax.rem(tp + n_tp - s, n_tp) * rows, rows)

    def y_copy(s):
        return remote(qs.at[0, s], qprev.at[s], y_send.at[s], y_recv.at[s], ahead(8), tp)

    def z_copy(dz, s, src):
        return remote(
            src, qs.at[2 * dz, s], z_send.at[dz - 1, s], z_recv.at[dz - 1, s], z_peer(dz), tp
        )

    def p_copy(s, src):
        return remote(src, qs.at[1 + 6 * core, s], p_send.at[s], p_recv.at[s], mate, tp)

    def f_copy(dz, s):
        return remote(
            qs.at[2 * dz, s],
            qs.at[2 * dz + 1 - 2 * core, s],
            f_send.at[dz - 1, s],
            f_recv.at[dz - 1, s],
            mate,
            tp,
        )

    length = plan_ref[0, req]
    for k in range(1, spread):
        length += plan_ref[k, req]
    coarse = length // 128
    fine = coarse_rows + length - coarse * 128

    def stage(blocks, at, n):
        width = depth // 5
        acc[: n * rows] = jnp.zeros((n * rows, acc.shape[1]), jnp.float32)

        def block(b, carry):
            cols = pl.ds(pl.multiple_of(b * width, width), width)
            left_side = xs[at : at + n, :, cols].reshape(n * rows, width)
            acc[: n * rows] += jnp.dot(
                left_side, w[cols, :], preferred_element_type=jnp.float32
            )
            return carry

        lax.fori_loop(0, 5, block, 0)
        c_a, s_a = tab[0, pl.ds(coarse, 1), :], tab[1, pl.ds(coarse, 1), :]
        c_b, s_b = tab[0, pl.ds(fine, 1), :], tab[1, pl.ds(fine, 1), :]
        c_l, s_l = c_a * c_b - s_a * s_b, s_a * c_b + c_a * s_b
        for i, s in enumerate(blocks):
            here = pl.ds(first_row(s), rows)
            there = pl.ds(pl.multiple_of(coarse_rows + first_row(s), 8), rows)
            c_t, s_t = tab[0, there, :], tab[1, there, :]
            cosine, sine = c_t * c_l - s_t * s_l, s_t * c_l + c_t * s_l

            def turned(col, gain):
                head = acc[i * rows : (i + 1) * rows, col : col + hd]
                mean = jnp.mean(head * head, axis=-1, keepdims=True)
                head = head * lax.rsqrt(mean + norm_eps) * gain
                return (head * cosine + pltpu.roll(head, hd // 2, 1) * sine).astype(
                    jnp.bfloat16
                )

            for h in range(heads):
                qs[0, s, h * rows : (h + 1) * rows] = turned(h * hd, q_gain)
            nk[here, :] = turned(qw, k_gain)
            nv[here, :hd] = acc[i * rows : (i + 1) * rows, qw + hd :].astype(jnp.bfloat16)
            y_copy(s).start()
            for dz in dzs:

                @pl.when(z + dz < 4)
                def _():
                    z_copy(dz, s, qs.at[0, s]).start()

            @pl.when(core == 0)
            def _():
                p_copy(s, qs.at[0, s]).start()

    def relay(s):
        y_copy(s).wait_recv()
        for dz in dzs:

            @pl.when(z + dz >= 4)
            def _():
                z_copy(dz, s, qprev.at[s]).start()

        @pl.when(core == 1)
        def _():
            p_copy(s, qprev.at[s]).start()

    def pass_on(s):
        for dz in dzs:
            z_copy(dz, s, qprev.at[s]).wait_recv()
            f_copy(dz, s).start()

    def arrive(s):
        p_copy(s, qprev.at[s]).wait_recv()
        for dz in dzs:
            f_copy(dz, s).wait_recv()

    def softmax(scores, values):
        top = jnp.max(scores, axis=1, keepdims=True)
        weights = jnp.exp2(scores - top).astype(jnp.bfloat16)
        both = jnp.dot(weights, values, preferred_element_type=jnp.float32)
        return both[:, :hd], both[:, hd:], top

    def dot_t(a, b):
        return lax.dot_general(a, b, (((1,), (1,)), ((), ())), preferred_element_type=jnp.float32)

    lanes = lax.broadcasted_iota(jnp.int32, (rows, hd), 1)

    def settle(parts):
        summed = jnp.concatenate([one[0] for one in parts], axis=0)
        mass = jnp.concatenate([one[1] for one in parts], axis=0)
        top = jnp.concatenate([one[2] for one in parts], axis=0)
        some = mass > 0
        value = jnp.where(some, summed / mass, 0.0).astype(jnp.bfloat16)
        level = jnp.where(some, top + jnp.log2(mass), NEG)
        table = jnp.full((rows, hd), NEG, jnp.float32)
        for h in range(heads):
            table = jnp.where(lanes == h, level[h * rows : (h + 1) * rows], table)
        table = jnp.concatenate([table, jnp.zeros_like(table)], axis=0)
        return value, jnp.transpose(table)[:8]

    def attend(blocks, first, last, unroll):
        sub = tall // 2

        def piece(k, carry):
            keys = kx[pl.ds(pl.multiple_of(k * cap, cap), cap), :]
            values = vx[pl.ds(pl.multiple_of(k * cap, cap), cap), :]
            scores = [
                dot_t(qs[k, s, n * sub : (n + 1) * sub], keys) for s in blocks for n in range(2)
            ]
            done = [softmax(one, values) for one in scores]
            for i, s in enumerate(blocks):
                obuf[k, s], stat[k, s] = settle(done[2 * i : 2 * i + 2])
            return carry

        lax.fori_loop(first, last, piece, 0, unroll=unroll)

    def attend_new(s):
        scores = dot_t(qs[0, s], nk[...])
        row = lax.broadcasted_iota(jnp.int32, scores.shape, 0)
        row = first_row(s) + jnp.bitwise_and(row, rows - 1)
        col = lax.broadcasted_iota(jnp.int32, scores.shape, 1)
        scores = jnp.where(row >= col, scores, NEG)
        onew[s], stat[spread, s] = settle([softmax(scores, nv[...])])

    def prepare():
        def piece(k, carry):
            at = pl.ds(pl.multiple_of(k * cap, cap), cap)
            count = plan_ref[k, lax.rem(req + n_req - k, n_req)]
            row = lax.broadcasted_iota(jnp.int32, (cap, hd), 0)
            ok = row < count
            keys = kx[at, :]
            kx[at, :] = jnp.where(ok, keys, jnp.broadcast_to(keys[0:1], keys.shape))
            vx[at, :hd] = jnp.where(ok, vx[at, :hd], jnp.zeros((cap, hd), jnp.bfloat16))
            vx[at, hd:] = jnp.where(ok, 1.0, 0.0).astype(jnp.bfloat16)
            return carry

        lax.fori_loop(0, spread, piece, 0)
        nv[:, hd:] = jnp.ones((nv.shape[0], hd), jnp.bfloat16)

    def m_copy(dz, s):
        return remote(
            obuf.at[2 * dz - 1 + 2 * core, s],
            mbuf.at[dz - 1, s],
            m_send.at[dz - 1, s],
            m_recv.at[dz - 1, s],
            mate,
            tp,
        )

    def ms_copy(dz, s):
        return remote(
            stat.at[2 * dz - 1 + 2 * core, s],
            mst.at[dz - 1, s],
            ms_send.at[dz - 1, s],
            ms_recv.at[dz - 1, s],
            mate,
            tp,
        )

    def d_copy(s):
        return remote(obuf.at[lone, s], dbuf.at[s], d_send.at[s], d_recv.at[s], ahead(-lone), tp)

    def ds_copy(s):
        return remote(stat.at[lone, s], dst.at[s], ds_send.at[s], ds_recv.at[s], ahead(-lone), tp)

    def r_copy(dz, s, part):
        return remote(
            sbuf.at[dz - 1, s, part],
            rbuf.at[dz - 1, s, part],
            r_send.at[dz - 1, s, part],
            r_recv.at[dz - 1, s, part],
            ahead(-2 * dz),
            tp,
        )

    def rs_copy(dz, s):
        return remote(
            sst.at[dz - 1, s],
            rst.at[dz - 1, s],
            rs_send.at[dz - 1, s],
            rs_recv.at[dz - 1, s],
            ahead(-2 * dz),
            tp,
        )

    def exchange(s):
        for dz in dzs:
            ms_copy(dz, s).start()
            m_copy(dz, s).start()
        ds_copy(s).start()
        d_copy(s).start()

    def columns(pieces):
        pad = jnp.zeros((128 - 8 * len(pieces), hd), jnp.float32)
        return jnp.transpose(jnp.concatenate(pieces + [pad], axis=0))[:rows]

    def pair_up(s):
        for dz in dzs:
            ms_copy(dz, s).wait_recv()
        shares = []
        for dz in dzs:
            mine, other = stat[2 * dz, s], mst[dz - 1, s]
            top = jnp.maximum(mine, other)
            mine, other = jnp.exp2(mine - top), jnp.exp2(other - top)
            mass = mine + other
            sst[dz - 1, s] = top + jnp.log2(mass)
            shares += [mine / mass, other / mass]
        table = columns(shares)
        for dz in dzs:
            m_copy(dz, s).wait_recv()
            for h in range(heads):
                at = slice(h * rows, (h + 1) * rows)
                i, j = 16 * (dz - 1) + h, 16 * (dz - 1) + 8 + h
                both = widen(obuf[2 * dz, s, at]) * table[:, i : i + 1]
                both += widen(mbuf[dz - 1, s, at]) * table[:, j : j + 1]
                both = both.astype(jnp.bfloat16)
                for part in range(2):
                    sbuf[dz - 1, s, part, h * half : (h + 1) * half] = both[
                        part * half : (part + 1) * half
                    ]
            rs_copy(dz, s).start()

    def give_back(s, part):
        for dz in dzs:
            r_copy(dz, s, part).start()

    def levels(s):
        ds_copy(s).wait_recv()
        d_copy(s).wait_recv()
        for dz in dzs:
            rs_copy(dz, s).wait_recv()
        tops = [stat[spread, s], stat[0, s], dst[s]] + [rst[dz - 1, s] for dz in dzs]
        top = functools.reduce(jnp.maximum, tops)
        masses = [jnp.exp2(one - top) for one in tops]
        mass = functools.reduce(jnp.add, masses)
        return columns([one / mass for one in masses])

    def merged(s, part, table):
        for dz in dzs:
            r_copy(dz, s, part).wait_recv()
        table = table[part * half : (part + 1) * half]
        heads_out = []
        for h in range(heads):
            at = slice(h * rows + part * half, h * rows + (part + 1) * half)
            sources = [onew[s, at], obuf[0, s, at], dbuf[s, at]]
            sources += [rbuf[dz - 1, s, part, h * half : (h + 1) * half] for dz in dzs]
            value = jnp.zeros((half, hd), jnp.float32)
            for n, source in enumerate(sources):
                i = 8 * n + h
                value += widen(source) * table[:, i : i + 1]
            heads_out.append(value.astype(jnp.bfloat16))
        return jnp.concatenate(heads_out, axis=1)

    def both_halves(s):
        table = levels(s)
        return jnp.concatenate([merged(s, 0, table), merged(s, 1, table)], axis=0)

    def project(attended, store):
        width = depth // 5

        def tile(b, carry):
            at = pl.ds(pl.multiple_of(b * width, width), width)
            store(at, jnp.dot(attended, wo[:, at], preferred_element_type=jnp.float32))
            return carry

        lax.fori_loop(0, 5, tile, 0)

    def x_copy(index, src, target_ref, target):
        return remote(src, target_ref, x_send.at[index], x_recv.at[index], req, target)

    width = depth // 5
    tiles = [slice(n * width, (n + 1) * width) for n in range(5)]
    x_far_low = [
        x_copy(n, psend.at[1, low, at], pre.at[0, :, at], right) for n, at in enumerate(tiles)
    ]
    x_far_high = [
        x_copy(5 + n, psend.at[1, high, at], pre.at[1, :, at], left)
        for n, at in enumerate(tiles)
    ]
    x_join_right = [
        x_copy(10 + n, psend.at[2, low, at], full.at[0, low, at], right)
        for n, at in enumerate(tiles)
    ]
    x_join_left = [
        x_copy(15 + n, psend.at[0, high, at], full.at[1, high, at], left)
        for n, at in enumerate(tiles)
    ]
    x_right = [
        x_copy(20 + n, psend.at[2, high, at], full.at[0, high, at], right)
        for n, at in enumerate(tiles)
    ]
    x_left = [
        x_copy(25 + n, psend.at[0, low, at], full.at[1, low, at], left)
        for n, at in enumerate(tiles)
    ]

    def join(index, part, slot, at):
        psend[index, part, at] = (
            widen(psend[index, part, at]) + widen(pre[slot, :, at])
        ).astype(jnp.bfloat16)

    for copy in load_w:
        copy.wait()
    load_tab.wait()
    for copy in load_kv:
        copy.start()
    load_wo.start()
    stage((0,), 0, 1)
    ag_copies[0].wait_recv()
    ag_copies[4].start()
    ag_copies[1].wait_recv()
    ag_copies[5].start()
    relay(0)
    for copy in load_kv:
        copy.wait()
    prepare()
    pass_on(0)
    ag_copies[2].wait_recv()
    ag_copies[3].wait_recv()
    stage((1, 3), 1, 2)
    arrive(0)
    attend((0,), 0, 4, 2)
    relay(1)
    relay(3)
    ag_copies[4].wait_recv()
    ag_copies[5].wait_recv()
    stage((2,), 3, 1)
    attend((0,), 4, 8, 2)
    exchange(0)
    pass_on(1)
    pass_on(3)
    relay(2)
    arrive(1)
    arrive(3)
    attend((1, 3), 0, 4, 1)
    pass_on(2)
    pair_up(0)
    give_back(0, 0)
    give_back(0, 1)
    attend((1, 3), 4, 8, 1)
    exchange(1)
    exchange(3)
    arrive(2)
    attend((2,), 0, 2, 2)
    pair_up(1)
    give_back(1, 0)
    pair_up(3)
    give_back(3, 1)
    give_back(1, 1)
    give_back(3, 0)
    attend((2,), 2, 8, 2)
    exchange(2)
    load_wo.wait()
    attend_new(1)
    attend_new(3)
    attend_new(2)
    pair_up(2)
    give_back(2, 0)
    give_back(2, 1)
    table_1, table_3 = levels(1), levels(3)
    attended = jnp.concatenate([merged(1, 0, table_1), merged(3, 1, table_3)], axis=0)
    for n, at in enumerate(tiles):
        value = jnp.dot(attended, wo[:, at], preferred_element_type=jnp.float32)
        psend[0, low, at] = value[:half].astype(jnp.bfloat16)
        psend[2, high, at] = value[half:].astype(jnp.bfloat16)
        if n:
            x_left[n - 1].start()
            x_right[n - 1].start()
    x_left[-1].start()
    x_right[-1].start()

    def store_rest(at, value):
        psend[0, high, at] = value[:half].astype(jnp.bfloat16)
        psend[2, low, at] = value[half:].astype(jnp.bfloat16)

    attended = jnp.concatenate([merged(1, 1, table_1), merged(3, 0, table_3)], axis=0)
    project(attended, store_rest)
    attended_2 = both_halves(2)
    for n, at in enumerate(tiles):
        value = jnp.dot(attended_2, wo[:, at], preferred_element_type=jnp.float32)
        psend[1, :, at] = value.astype(jnp.bfloat16)
        if n:
            x_far_low[n - 1].start()
            x_far_high[n - 1].start()
    x_far_low[-1].start()
    x_far_high[-1].start()

    def keep(at, value):
        total[:, at] = widen(tok[:, at]) + widen(value.astype(jnp.bfloat16))

    attend_new(0)
    project(both_halves(0), keep)
    for n, at in enumerate(tiles):
        x_far_low[n].wait_recv()
        join(2, low, 0, at)
        x_far_high[n].wait_recv()
        join(0, high, 1, at)
        x_join_right[n].start()
        x_join_left[n].start()
    for n, at in enumerate(tiles):
        x_right[n].wait_recv()
        x_left[n].wait_recv()
        x_join_right[n].wait_recv()
        x_join_left[n].wait_recv()
        out_ref[:, at] = (
            total[:, at] + widen(full[0, :, at]) + widen(full[1, :, at])
        ).astype(jnp.bfloat16)

    for copy in ag_copies + x_far_low + x_far_high + x_join_left + x_join_right + x_left + x_right:
        copy.wait_send()
    for s in range(4):
        y_copy(s).wait_send()
        p_copy(s, qprev.at[s]).wait_send()
        d_copy(s).wait_send()
        ds_copy(s).wait_send()
        for dz in dzs:
            z_copy(dz, s, qprev.at[s]).wait_send()
            f_copy(dz, s).wait_send()
            m_copy(dz, s).wait_send()
            ms_copy(dz, s).wait_send()
            r_copy(dz, s, 0).wait_send()
            r_copy(dz, s, 1).wait_send()
            rs_copy(dz, s).wait_send()


def turn_tables(head_dim, count):
    freqs = rope_base ** (-np.arange(head_dim // 2) * 2.0 / head_dim)
    steps = np.concatenate([128.0 * np.arange(coarse_rows), np.arange(count)])
    angles = steps[:, None] * freqs[None, :]
    cosine, sine = np.cos(angles), np.sin(angles)
    return np.stack(
        [np.concatenate([cosine, cosine], axis=1), np.concatenate([-sine, sine], axis=1)]
    ).astype(np.float32)


def on_device(
    tokens,
    norm_gain,
    w_query,
    w_key,
    w_value,
    query_gain,
    key_gain,
    w_out,
    cache_keys,
    cache_values,
    cache_plan,
):
    hd = query_gain.shape[0]
    rows, depth = tokens.shape
    qw = w_query.shape[1]
    spread = cache_plan.shape[1]
    n_tp = lax.axis_size("tp")
    count = rows * n_tp
    tall = qw // hd * rows
    tables = jnp.asarray(turn_tables(hd, max(count, 128)))
    vm = pl.BlockSpec(memory_space=pltpu.VMEM)
    hbm = pl.BlockSpec(memory_space=pltpu.HBM)
    bf16, f32 = jnp.bfloat16, jnp.float32
    dma = pltpu.SemaphoreType.DMA
    return pl.pallas_call(
        functools.partial(kernel, hd ** (-0.5) * log2e),
        out_shape=jax.ShapeDtypeStruct((rows, depth), bf16),
        in_specs=[pl.BlockSpec(memory_space=pltpu.SMEM)] + [hbm] * 11,
        out_specs=vm,
        scratch_shapes=[
            pltpu.VMEM(tables.shape, f32),
            pltpu.VMEM((depth // hd, hd), bf16),
            pltpu.VMEM((2, 1, hd), bf16),
            pltpu.VMEM((rows, depth), bf16),
            pltpu.VMEM((n_tp, rows, depth), bf16),
            pltpu.VMEM((depth, qw + 2 * hd), bf16),
            pltpu.VMEM(w_out.shape, bf16),
            pltpu.VMEM((2 * rows, qw + 2 * hd), f32),
            pltpu.VMEM(cache_keys.shape, bf16),
            pltpu.VMEM((cache_keys.shape[0], 2 * hd), bf16),
            pltpu.VMEM((count, hd), bf16),
            pltpu.VMEM((count, 2 * hd), bf16),
            pltpu.VMEM((spread, n_tp, tall, hd), bf16),
            pltpu.VMEM((n_tp, tall, hd), bf16),
            pltpu.VMEM((spread, n_tp, tall, hd), bf16),
            pltpu.VMEM((n_tp, tall, hd), bf16),
            pltpu.VMEM((spread + 1, n_tp, 8, hd), f32),
            pltpu.VMEM((3, n_tp, tall, hd), bf16),
            pltpu.VMEM((3, n_tp, 8, hd), f32),
            pltpu.VMEM((n_tp, tall, hd), bf16),
            pltpu.VMEM((n_tp, 8, hd), f32),
            pltpu.VMEM((3, n_tp, 2, tall // 2, hd), bf16),
            pltpu.VMEM((3, n_tp, 8, hd), f32),
            pltpu.VMEM((3, n_tp, 2, tall // 2, hd), bf16),
            pltpu.VMEM((3, n_tp, 8, hd), f32),
            pltpu.VMEM((3, rows, depth), bf16),
            pltpu.VMEM((2, rows // 2, depth), bf16),
            pltpu.VMEM((2, rows, depth), bf16),
            pltpu.VMEM((rows, depth), f32),
            dma((12,)),
            dma((6,)),
            dma((6,)),
            dma((4,)),
            dma((4,)),
            dma((3, 4)),
            dma((3, 4)),
            dma((4,)),
            dma((4,)),
            dma((3, 4)),
            dma((3, 4)),
            dma((3, 4)),
            dma((3, 4)),
            dma((3, 4)),
            dma((3, 4)),
            dma((4,)),
            dma((4,)),
            dma((4,)),
            dma((4,)),
            dma((3, 4, 2)),
            dma((3, 4, 2)),
            dma((3, 4)),
            dma((3, 4)),
            dma((30,)),
            dma((30,)),
        ],
        compiler_params=pltpu.CompilerParams(
            collective_id=0, has_side_effects=True, vmem_limit_bytes=64 * 1000 * 1000
        ),
    )(
        cache_plan.T,
        norm_gain.reshape(depth // hd, hd),
        query_gain.reshape(1, hd),
        key_gain.reshape(1, hd),
        tables,
        tokens,
        w_query,
        w_key,
        w_value,
        w_out,
        cache_keys,
        cache_values,
    )


def solution(mesh):
    placed = (
        P(("req", "tp"), None),
        P(),
        P(None, "tp"),
        P(None, "tp"),
        P(None, "tp"),
        P(),
        P(),
        P("tp", None),
        P("req", "tp"),
        P("req", "tp"),
        P(),
    )
    return jax.shard_map(
        on_device, mesh=mesh, in_specs=placed, out_specs=P(("req", "tp"), None), check_vma=False
    )
```

```python
import functools
import jax
import jax.numpy as jnp
import numpy as np
from jax import lax
from jax.experimental import pallas as pl
from jax.experimental.pallas import tpu as pltpu
from jax.sharding import PartitionSpec as P

norm_eps = 1e-06
rope_base = 1000000.0
log2e = 1.4426950408889634
NEG = -1e30
MESH = pl.DeviceIdType.MESH
coarse_rows = 136


def widen(value):
    return value.astype(jnp.float32)


def remote(src, dst, send, recv, req, tp):
    return pltpu.make_async_remote_copy(
        src_ref=src,
        dst_ref=dst,
        send_sem=send,
        recv_sem=recv,
        device_id=(req, tp),
        device_id_type=MESH,
    )


def kernel(
    score_scale,
    plan_ref,
    ng_hbm,
    qg_hbm,
    kg_hbm,
    tab_hbm,
    tok_hbm,
    wq_hbm,
    wk_hbm,
    wv_hbm,
    wo_hbm,
    k_hbm,
    v_hbm,
    out_ref,
    tab,
    gains,
    head_gains,
    tok,
    xs,
    w,
    wo,
    acc,
    kx,
    vx,
    nk,
    nv,
    qs,
    qprev,
    obuf,
    onew,
    stat,
    mbuf,
    mst,
    dbuf,
    dst,
    sbuf,
    sst,
    rbuf,
    rst,
    psend,
    pre,
    full,
    total,
    load_sem,
    ag_send,
    ag_recv,
    y_send,
    y_recv,
    z_send,
    z_recv,
    p_send,
    p_recv,
    f_send,
    f_recv,
    m_send,
    m_recv,
    ms_send,
    ms_recv,
    d_send,
    d_recv,
    ds_send,
    ds_recv,
    r_send,
    r_recv,
    rs_send,
    rs_recv,
    x_send,
    x_recv,
):
    req, tp = lax.axis_index("req"), lax.axis_index("tp")
    n_req, n_tp = lax.axis_size("req"), lax.axis_size("tp")
    core = lax.rem(req, 2)
    z = lax.rem(req // 2, 4)
    plane = req - 2 * z - core
    rows, depth = tok.shape
    half = rows // 2
    spread = plan_ref.shape[0]
    cap = kx.shape[0] // spread
    hd = kx.shape[1]
    qw = wo.shape[0]
    heads = qw // hd
    tall = heads * rows
    right, left = lax.rem(tp + 1, n_tp), lax.rem(tp + n_tp - 1, n_tp)
    mate = req + 1 - 2 * core
    lone = 7 - 6 * core
    dzs = (1, 2, 3)

    def ahead(steps):
        return lax.rem(req + n_req + steps, n_req)

    def z_peer(dz):
        return plane + 2 * lax.rem(z + dz, 4) + core

    def load(index, src, target):
        return pltpu.make_async_copy(src, target, load_sem.at[index])

    low, high = slice(0, half), slice(half, rows)
    load_tok = [load(0, tok_hbm.at[low], tok.at[low]), load(8, tok_hbm.at[high], tok.at[high])]
    lanes_of = depth // hd
    load_gains = [
        load(9, ng_hbm, gains),
        load(10, qg_hbm, head_gains.at[0]),
        load(11, kg_hbm, head_gains.at[1]),
    ]
    load_w = [
        load(1, wq_hbm, w.at[:, :qw]),
        load(2, wk_hbm, w.at[:, qw : qw + hd]),
        load(3, wv_hbm, w.at[:, qw + hd :]),
    ]
    load_tab = load(4, tab_hbm, tab)
    load_kv = [load(5, k_hbm, kx), load(6, v_hbm, vx.at[:, :hd])]
    load_wo = load(7, wo_hbm, wo)
    for copy in load_tok + load_gains + load_w:
        copy.start()
    load_tab.start()

    barrier = pltpu.get_barrier_semaphore()
    partners = [(req, right), (req, left), (mate, tp), (ahead(14 * core - 7), tp)]
    partners += [(ahead(steps), tp) for steps in (8, -8, 2, 4, 6, -2, -4, -6)]
    partners += [(z_peer(dz), tp) for dz in dzs]
    for where in partners:
        pl.semaphore_signal(barrier, inc=1, device_id=where, device_id_type=MESH)

    for copy in load_gains:
        copy.wait()
    gain = widen(gains[...])
    q_gain = widen(head_gains[0]) * score_scale
    k_gain = widen(head_gains[1])

    def normalize(part, load_part):
        load_part.wait()
        value = widen(tok[part])
        scale = lax.rsqrt(jnp.mean(value * value, axis=-1, keepdims=True) + norm_eps)
        for n in range(lanes_of):
            at = slice(n * hd, (n + 1) * hd)
            xs[0, part, at] = (value[:, at] * scale * gain[n : n + 1]).astype(jnp.bfloat16)

    normalize(low, load_tok[0])
    pl.semaphore_wait(barrier, len(partners))

    def ag(index, at_from, at_to, part, target):
        return remote(
            xs.at[at_from, part],
            xs.at[at_to, part],
            ag_send.at[index],
            ag_recv.at[index],
            req,
            target,
        )

    ag_copies = [
        ag(0, 0, 1, low, right),
        ag(1, 0, 2, high, left),
        ag(2, 0, 1, high, right),
        ag(3, 0, 2, low, left),
        ag(4, 1, 3, low, right),
        ag(5, 2, 3, high, left),
    ]
    ag_copies[0].start()
    normalize(high, load_tok[1])
    for copy in ag_copies[1:4]:
        copy.start()

    def first_row(s):
        return pl.multiple_of(lax.rem(tp + n_tp - s, n_tp) * rows, rows)

    def y_copy(s):
        return remote(qs.at[0, s], qprev.at[s], y_send.at[s], y_recv.at[s], ahead(8), tp)

    def z_copy(dz, s, src):
        return remote(
            src, qs.at[2 * dz, s], z_send.at[dz - 1, s], z_recv.at[dz - 1, s], z_peer(dz), tp
        )

    def p_copy(s, src):
        return remote(src, qs.at[1 + 6 * core, s], p_send.at[s], p_recv.at[s], mate, tp)

    def f_copy(dz, s):
        return remote(
            qs.at[2 * dz, s],
            qs.at[2 * dz + 1 - 2 * core, s],
            f_send.at[dz - 1, s],
            f_recv.at[dz - 1, s],
            mate,
            tp,
        )

    length = plan_ref[0, req]
    for k in range(1, spread):
        length += plan_ref[k, req]
    coarse = length // 128
    fine = coarse_rows + length - coarse * 128

    def stage(blocks, at, n):
        width = depth // 5
        acc[: n * rows] = jnp.zeros((n * rows, acc.shape[1]), jnp.float32)

        def block(b, carry):
            cols = pl.ds(pl.multiple_of(b * width, width), width)
            left_side = xs[at : at + n, :, cols].reshape(n * rows, width)
            acc[: n * rows] += jnp.dot(
                left_side, w[cols, :], preferred_element_type=jnp.float32
            )
            return carry

        lax.fori_loop(0, 5, block, 0)
        c_a, s_a = tab[0, pl.ds(coarse, 1), :], tab[1, pl.ds(coarse, 1), :]
        c_b, s_b = tab[0, pl.ds(fine, 1), :], tab[1, pl.ds(fine, 1), :]
        c_l, s_l = c_a * c_b - s_a * s_b, s_a * c_b + c_a * s_b
        for i, s in enumerate(blocks):
            here = pl.ds(first_row(s), rows)
            there = pl.ds(pl.multiple_of(coarse_rows + first_row(s), 8), rows)
            c_t, s_t = tab[0, there, :], tab[1, there, :]
            cosine, sine = c_t * c_l - s_t * s_l, s_t * c_l + c_t * s_l

            def turned(col, gain):
                head = acc[i * rows : (i + 1) * rows, col : col + hd]
                mean = jnp.mean(head * head, axis=-1, keepdims=True)
                head = head * lax.rsqrt(mean + norm_eps) * gain
                return (head * cosine + pltpu.roll(head, hd // 2, 1) * sine).astype(
                    jnp.bfloat16
                )

            for h in range(heads):
                qs[0, s, h * rows : (h + 1) * rows] = turned(h * hd, q_gain)
            nk[here, :] = turned(qw, k_gain)
            nv[here, :hd] = acc[i * rows : (i + 1) * rows, qw + hd :].astype(jnp.bfloat16)
            y_copy(s).start()
            for dz in dzs:

                @pl.when(z + dz < 4)
                def _():
                    z_copy(dz, s, qs.at[0, s]).start()

            @pl.when(core == 0)
            def _():
                p_copy(s, qs.at[0, s]).start()

    def relay(s):
        y_copy(s).wait_recv()
        for dz in dzs:

            @pl.when(z + dz >= 4)
            def _():
                z_copy(dz, s, qprev.at[s]).start()

        @pl.when(core == 1)
        def _():
            p_copy(s, qprev.at[s]).start()

    def pass_on(s):
        for dz in dzs:
            z_copy(dz, s, qprev.at[s]).wait_recv()
            f_copy(dz, s).start()

    def arrive(s):
        p_copy(s, qprev.at[s]).wait_recv()
        for dz in dzs:
            f_copy(dz, s).wait_recv()

    def softmax(scores, values):
        top = jnp.max(scores, axis=1, keepdims=True)
        weights = jnp.exp2(scores - top).astype(jnp.bfloat16)
        both = jnp.dot(weights, values, preferred_element_type=jnp.float32)
        return both[:, :hd], both[:, hd:], top

    def dot_t(a, b):
        return lax.dot_general(a, b, (((1,), (1,)), ((), ())), preferred_element_type=jnp.float32)

    lanes = lax.broadcasted_iota(jnp.int32, (rows, hd), 1)

    def settle(parts):
        summed = jnp.concatenate([one[0] for one in parts], axis=0)
        mass = jnp.concatenate([one[1] for one in parts], axis=0)
        top = jnp.concatenate([one[2] for one in parts], axis=0)
        some = mass > 0
        value = jnp.where(some, summed / mass, 0.0).astype(jnp.bfloat16)
        level = jnp.where(some, top + jnp.log2(mass), NEG)
        table = jnp.full((rows, hd), NEG, jnp.float32)
        for h in range(heads):
            table = jnp.where(lanes == h, level[h * rows : (h + 1) * rows], table)
        table = jnp.concatenate([table, jnp.zeros_like(table)], axis=0)
        return value, jnp.transpose(table)[:8]

    def attend(blocks, first, last, unroll):
        sub = tall // 2

        def piece(n, carry):
            k = 2 * lax.rem(n, 4) + 1 - n // 4
            keys = kx[pl.ds(pl.multiple_of(k * cap, cap), cap), :]
            values = vx[pl.ds(pl.multiple_of(k * cap, cap), cap), :]
            scores = [
                dot_t(qs[k, s, n * sub : (n + 1) * sub], keys) for s in blocks for n in range(2)
            ]
            done = [softmax(one, values) for one in scores]
            for i, s in enumerate(blocks):
                obuf[k, s], stat[k, s] = settle(done[2 * i : 2 * i + 2])
            return carry

        lax.fori_loop(first, last, piece, 0, unroll=unroll)

    def attend_new(s):
        scores = dot_t(qs[0, s], nk[...])
        row = lax.broadcasted_iota(jnp.int32, scores.shape, 0)
        row = first_row(s) + jnp.bitwise_and(row, rows - 1)
        col = lax.broadcasted_iota(jnp.int32, scores.shape, 1)
        scores = jnp.where(row >= col, scores, NEG)
        onew[s], stat[spread, s] = settle([softmax(scores, nv[...])])

    def prepare():
        def piece(k, carry):
            at = pl.ds(pl.multiple_of(k * cap, cap), cap)
            count = plan_ref[k, lax.rem(req + n_req - k, n_req)]
            row = lax.broadcasted_iota(jnp.int32, (cap, hd), 0)
            ok = row < count
            keys = kx[at, :]
            kx[at, :] = jnp.where(ok, keys, jnp.broadcast_to(keys[0:1], keys.shape))
            vx[at, :hd] = jnp.where(ok, vx[at, :hd], jnp.zeros((cap, hd), jnp.bfloat16))
            vx[at, hd:] = jnp.where(ok, 1.0, 0.0).astype(jnp.bfloat16)
            return carry

        lax.fori_loop(0, spread, piece, 0)
        nv[:, hd:] = jnp.ones((nv.shape[0], hd), jnp.bfloat16)

    def m_copy(dz, s):
        return remote(
            obuf.at[2 * dz - 1 + 2 * core, s],
            mbuf.at[dz - 1, s],
            m_send.at[dz - 1, s],
            m_recv.at[dz - 1, s],
            mate,
            tp,
        )

    def ms_copy(dz, s):
        return remote(
            stat.at[2 * dz - 1 + 2 * core, s],
            mst.at[dz - 1, s],
            ms_send.at[dz - 1, s],
            ms_recv.at[dz - 1, s],
            mate,
            tp,
        )

    def d_copy(s):
        return remote(obuf.at[lone, s], dbuf.at[s], d_send.at[s], d_recv.at[s], ahead(-lone), tp)

    def ds_copy(s):
        return remote(stat.at[lone, s], dst.at[s], ds_send.at[s], ds_recv.at[s], ahead(-lone), tp)

    def r_copy(dz, s, part):
        return remote(
            sbuf.at[dz - 1, s, part],
            rbuf.at[dz - 1, s, part],
            r_send.at[dz - 1, s, part],
            r_recv.at[dz - 1, s, part],
            ahead(-2 * dz),
            tp,
        )

    def rs_copy(dz, s):
        return remote(
            sst.at[dz - 1, s],
            rst.at[dz - 1, s],
            rs_send.at[dz - 1, s],
            rs_recv.at[dz - 1, s],
            ahead(-2 * dz),
            tp,
        )

    def exchange(s):
        for dz in dzs:
            ms_copy(dz, s).start()
            m_copy(dz, s).start()
        ds_copy(s).start()
        d_copy(s).start()

    def columns(pieces):
        pad = jnp.zeros((128 - 8 * len(pieces), hd), jnp.float32)
        return jnp.transpose(jnp.concatenate(pieces + [pad], axis=0))[:rows]

    def pair_up(s):
        for dz in dzs:
            ms_copy(dz, s).wait_recv()
        shares = []
        for dz in dzs:
            mine, other = stat[2 * dz, s], mst[dz - 1, s]
            top = jnp.maximum(mine, other)
            mine, other = jnp.exp2(mine - top), jnp.exp2(other - top)
            mass = mine + other
            sst[dz - 1, s] = top + jnp.log2(mass)
            shares += [mine / mass, other / mass]
        table = columns(shares)
        for dz in dzs:
            m_copy(dz, s).wait_recv()
            for h in range(heads):
                at = slice(h * rows, (h + 1) * rows)
                i, j = 16 * (dz - 1) + h, 16 * (dz - 1) + 8 + h
                both = widen(obuf[2 * dz, s, at]) * table[:, i : i + 1]
                both += widen(mbuf[dz - 1, s, at]) * table[:, j : j + 1]
                both = both.astype(jnp.bfloat16)
                for part in range(2):
                    sbuf[dz - 1, s, part, h * half : (h + 1) * half] = both[
                        part * half : (part + 1) * half
                    ]
            rs_copy(dz, s).start()

    def give_back(s, part):
        for dz in dzs:
            r_copy(dz, s, part).start()

    def levels(s):
        ds_copy(s).wait_recv()
        d_copy(s).wait_recv()
        for dz in dzs:
            rs_copy(dz, s).wait_recv()
        tops = [stat[spread, s], stat[0, s], dst[s]] + [rst[dz - 1, s] for dz in dzs]
        top = functools.reduce(jnp.maximum, tops)
        masses = [jnp.exp2(one - top) for one in tops]
        mass = functools.reduce(jnp.add, masses)
        return columns([one / mass for one in masses])

    def merged(s, part, table):
        for dz in dzs:
            r_copy(dz, s, part).wait_recv()
        table = table[part * half : (part + 1) * half]
        heads_out = []
        for h in range(heads):
            at = slice(h * rows + part * half, h * rows + (part + 1) * half)
            sources = [onew[s, at], obuf[0, s, at], dbuf[s, at]]
            sources += [rbuf[dz - 1, s, part, h * half : (h + 1) * half] for dz in dzs]
            value = jnp.zeros((half, hd), jnp.float32)
            for n, source in enumerate(sources):
                i = 8 * n + h
                value += widen(source) * table[:, i : i + 1]
            heads_out.append(value.astype(jnp.bfloat16))
        return jnp.concatenate(heads_out, axis=1)

    def both_halves(s):
        table = levels(s)
        return jnp.concatenate([merged(s, 0, table), merged(s, 1, table)], axis=0)

    def project(attended, store):
        width = depth // 5

        def tile(b, carry):
            at = pl.ds(pl.multiple_of(b * width, width), width)
            store(at, jnp.dot(attended, wo[:, at], preferred_element_type=jnp.float32))
            return carry

        lax.fori_loop(0, 5, tile, 0)

    def x_copy(index, src, target_ref, target):
        return remote(src, target_ref, x_send.at[index], x_recv.at[index], req, target)

    width = depth // 5
    tiles = [slice(n * width, (n + 1) * width) for n in range(5)]
    x_far_low = [
        x_copy(n, psend.at[1, low, at], pre.at[0, :, at], right) for n, at in enumerate(tiles)
    ]
    x_far_high = [
        x_copy(5 + n, psend.at[1, high, at], pre.at[1, :, at], left)
        for n, at in enumerate(tiles)
    ]
    x_join_right = [
        x_copy(10 + n, psend.at[2, low, at], full.at[0, low, at], right)
        for n, at in enumerate(tiles)
    ]
    x_join_left = [
        x_copy(15 + n, psend.at[0, high, at], full.at[1, high, at], left)
        for n, at in enumerate(tiles)
    ]
    x_right = [
        x_copy(20 + n, psend.at[2, high, at], full.at[0, high, at], right)
        for n, at in enumerate(tiles)
    ]
    x_left = [
        x_copy(25 + n, psend.at[0, low, at], full.at[1, low, at], left)
        for n, at in enumerate(tiles)
    ]

    def join(index, part, slot, at):
        psend[index, part, at] = (
            widen(psend[index, part, at]) + widen(pre[slot, :, at])
        ).astype(jnp.bfloat16)

    for copy in load_w:
        copy.wait()
    load_tab.wait()
    for copy in load_kv:
        copy.start()
    load_wo.start()
    stage((0,), 0, 1)
    ag_copies[0].wait_recv()
    ag_copies[4].start()
    ag_copies[1].wait_recv()
    ag_copies[5].start()
    relay(0)
    for copy in load_kv:
        copy.wait()
    prepare()
    pass_on(0)
    ag_copies[2].wait_recv()
    ag_copies[3].wait_recv()
    stage((1, 3), 1, 2)
    arrive(0)
    attend((0,), 0, 4, 2)
    relay(1)
    relay(3)
    ag_copies[4].wait_recv()
    ag_copies[5].wait_recv()
    stage((2,), 3, 1)
    exchange(0)
    attend((0,), 4, 8, 2)
    pass_on(1)
    pass_on(3)
    relay(2)
    attend_new(1)
    attend_new(3)
    arrive(1)
    arrive(3)
    attend((1, 3), 0, 4, 1)
    exchange(1)
    exchange(3)
    pass_on(2)
    pair_up(0)
    give_back(0, 0)
    give_back(0, 1)
    attend((1, 3), 4, 8, 1)
    pair_up(1)
    give_back(1, 0)
    pair_up(3)
    give_back(3, 1)
    give_back(1, 1)
    give_back(3, 0)
    arrive(2)
    attend((2,), 0, 4, 2)
    exchange(2)
    attend((2,), 4, 8, 2)
    load_wo.wait()
    pair_up(2)
    give_back(2, 0)
    give_back(2, 1)
    table_1, table_3 = levels(1), levels(3)
    attended = jnp.concatenate([merged(1, 0, table_1), merged(3, 1, table_3)], axis=0)
    for n, at in enumerate(tiles):
        value = jnp.dot(attended, wo[:, at], preferred_element_type=jnp.float32)
        psend[0, low, at] = value[:half].astype(jnp.bfloat16)
        psend[2, high, at] = value[half:].astype(jnp.bfloat16)
        if n:
            x_left[n - 1].start()
            x_right[n - 1].start()
    x_left[-1].start()
    x_right[-1].start()

    def store_rest(at, value):
        psend[0, high, at] = value[:half].astype(jnp.bfloat16)
        psend[2, low, at] = value[half:].astype(jnp.bfloat16)

    attended = jnp.concatenate([merged(1, 1, table_1), merged(3, 0, table_3)], axis=0)
    project(attended, store_rest)
    attend_new(2)
    attended_2 = both_halves(2)
    for n, at in enumerate(tiles):
        value = jnp.dot(attended_2, wo[:, at], preferred_element_type=jnp.float32)
        psend[1, :, at] = value.astype(jnp.bfloat16)
        if n:
            x_far_low[n - 1].start()
            x_far_high[n - 1].start()
    x_far_low[-1].start()
    x_far_high[-1].start()

    def keep(at, value):
        total[:, at] = widen(tok[:, at]) + widen(value.astype(jnp.bfloat16))

    attend_new(0)
    project(both_halves(0), keep)
    for n, at in enumerate(tiles):
        x_far_low[n].wait_recv()
        join(2, low, 0, at)
        x_far_high[n].wait_recv()
        join(0, high, 1, at)
        x_join_right[n].start()
        x_join_left[n].start()
    for n, at in enumerate(tiles):
        x_right[n].wait_recv()
        x_left[n].wait_recv()
        x_join_right[n].wait_recv()
        x_join_left[n].wait_recv()
        out_ref[:, at] = (
            total[:, at] + widen(full[0, :, at]) + widen(full[1, :, at])
        ).astype(jnp.bfloat16)

    for copy in ag_copies + x_far_low + x_far_high + x_join_left + x_join_right + x_left + x_right:
        copy.wait_send()
    for s in range(4):
        y_copy(s).wait_send()
        p_copy(s, qprev.at[s]).wait_send()
        d_copy(s).wait_send()
        ds_copy(s).wait_send()
        for dz in dzs:
            z_copy(dz, s, qprev.at[s]).wait_send()
            f_copy(dz, s).wait_send()
            m_copy(dz, s).wait_send()
            ms_copy(dz, s).wait_send()
            r_copy(dz, s, 0).wait_send()
            r_copy(dz, s, 1).wait_send()
            rs_copy(dz, s).wait_send()


def turn_tables(head_dim, count):
    freqs = rope_base ** (-np.arange(head_dim // 2) * 2.0 / head_dim)
    steps = np.concatenate([128.0 * np.arange(coarse_rows), np.arange(count)])
    angles = steps[:, None] * freqs[None, :]
    cosine, sine = np.cos(angles), np.sin(angles)
    return np.stack(
        [np.concatenate([cosine, cosine], axis=1), np.concatenate([-sine, sine], axis=1)]
    ).astype(np.float32)


def on_device(
    tokens,
    norm_gain,
    w_query,
    w_key,
    w_value,
    query_gain,
    key_gain,
    w_out,
    cache_keys,
    cache_values,
    cache_plan,
):
    hd = query_gain.shape[0]
    rows, depth = tokens.shape
    qw = w_query.shape[1]
    spread = cache_plan.shape[1]
    n_tp = lax.axis_size("tp")
    count = rows * n_tp
    tall = qw // hd * rows
    tables = jnp.asarray(turn_tables(hd, max(count, 128)))
    vm = pl.BlockSpec(memory_space=pltpu.VMEM)
    hbm = pl.BlockSpec(memory_space=pltpu.HBM)
    bf16, f32 = jnp.bfloat16, jnp.float32
    dma = pltpu.SemaphoreType.DMA
    return pl.pallas_call(
        functools.partial(kernel, hd ** (-0.5) * log2e),
        out_shape=jax.ShapeDtypeStruct((rows, depth), bf16),
        in_specs=[pl.BlockSpec(memory_space=pltpu.SMEM)] + [hbm] * 11,
        out_specs=vm,
        scratch_shapes=[
            pltpu.VMEM(tables.shape, f32),
            pltpu.VMEM((depth // hd, hd), bf16),
            pltpu.VMEM((2, 1, hd), bf16),
            pltpu.VMEM((rows, depth), bf16),
            pltpu.VMEM((n_tp, rows, depth), bf16),
            pltpu.VMEM((depth, qw + 2 * hd), bf16),
            pltpu.VMEM(w_out.shape, bf16),
            pltpu.VMEM((2 * rows, qw + 2 * hd), f32),
            pltpu.VMEM(cache_keys.shape, bf16),
            pltpu.VMEM((cache_keys.shape[0], 2 * hd), bf16),
            pltpu.VMEM((count, hd), bf16),
            pltpu.VMEM((count, 2 * hd), bf16),
            pltpu.VMEM((spread, n_tp, tall, hd), bf16),
            pltpu.VMEM((n_tp, tall, hd), bf16),
            pltpu.VMEM((spread, n_tp, tall, hd), bf16),
            pltpu.VMEM((n_tp, tall, hd), bf16),
            pltpu.VMEM((spread + 1, n_tp, 8, hd), f32),
            pltpu.VMEM((3, n_tp, tall, hd), bf16),
            pltpu.VMEM((3, n_tp, 8, hd), f32),
            pltpu.VMEM((n_tp, tall, hd), bf16),
            pltpu.VMEM((n_tp, 8, hd), f32),
            pltpu.VMEM((3, n_tp, 2, tall // 2, hd), bf16),
            pltpu.VMEM((3, n_tp, 8, hd), f32),
            pltpu.VMEM((3, n_tp, 2, tall // 2, hd), bf16),
            pltpu.VMEM((3, n_tp, 8, hd), f32),
            pltpu.VMEM((3, rows, depth), bf16),
            pltpu.VMEM((2, rows // 2, depth), bf16),
            pltpu.VMEM((2, rows, depth), bf16),
            pltpu.VMEM((rows, depth), f32),
            dma((12,)),
            dma((6,)),
            dma((6,)),
            dma((4,)),
            dma((4,)),
            dma((3, 4)),
            dma((3, 4)),
            dma((4,)),
            dma((4,)),
            dma((3, 4)),
            dma((3, 4)),
            dma((3, 4)),
            dma((3, 4)),
            dma((3, 4)),
            dma((3, 4)),
            dma((4,)),
            dma((4,)),
            dma((4,)),
            dma((4,)),
            dma((3, 4, 2)),
            dma((3, 4, 2)),
            dma((3, 4)),
            dma((3, 4)),
            dma((30,)),
            dma((30,)),
        ],
        compiler_params=pltpu.CompilerParams(
            collective_id=0, has_side_effects=True, vmem_limit_bytes=64 * 1000 * 1000
        ),
    )(
        cache_plan.T,
        norm_gain.reshape(depth // hd, hd),
        query_gain.reshape(1, hd),
        key_gain.reshape(1, hd),
        tables,
        tokens,
        w_query,
        w_key,
        w_value,
        w_out,
        cache_keys,
        cache_values,
    )


def solution(mesh):
    placed = (
        P(("req", "tp"), None),
        P(),
        P(None, "tp"),
        P(None, "tp"),
        P(None, "tp"),
        P(),
        P(),
        P("tp", None),
        P("req", "tp"),
        P("req", "tp"),
        P(),
    )
    return jax.shard_map(
        on_device, mesh=mesh, in_specs=placed, out_specs=P(("req", "tp"), None), check_vma=False
    )
```
